32 devices in a mesh: scen: 16 (over z, y, core), net: 2 (over x).
Axes of the slice: x: 2, y: 2, z: 4, core: 2. Of those that a mesh axis runs over, the one named last changes fastest.
Arguments:
- generation: float32 [16, 168, 4096], P('scen', None, 'net'), may hold values from 0 to 2
- charging: float32 [16, 168, 1024], P('scen', None, 'net'), may hold values from 0 to 0.5
- discharging: float32 [16, 168, 1024], P('scen', None, 'net'), may hold values from 0 to 0.5
- plant_capacity: float32 [4096], P('net'), may hold values from 1 to 3
- store_capacity: float32 [1024], P('net'), may hold values from 4 to 12
- dual_balance: float32 [16, 168], P('scen'), may hold values from -6 to 6
- dual_line: float32 [16, 168, 8192], P('scen', None, 'net'), may hold values from -6 to 6
- dual_headroom: float32 [16, 168, 4096], P('scen', None, 'net'), may hold values from 0 to 1
- dual_empty: float32 [16, 168, 1024], P('scen', None, 'net'), may hold values from -1 to 0
- dual_full: float32 [16, 168, 1024], P('scen', None, 'net'), may hold values from 0 to 1
- availability: float32 [16, 168, 4096], P('scen', None, 'net'), may hold values from 0.1 to 1
- demand: float32 [16, 168], P('scen'), may hold values from 0.5 to 1.5
- line_base: float32 [16, 168, 8192], P('scen', None, 'net'), may hold values from -6 to 6
- line_limit: float32 [8192], P('net'), may hold values from 0.5 to 2
- fuel_cost: float32 [4096], P('net'), may hold values from 0.1 to 2
- plant_cost: float32 [4096], P('net'), may hold values from 0.1 to 1
- store_cost: float32 [1024], P('net'), may hold values from 0.05 to 0.5
- self_loss: float32 [1024], P('net'), may hold values from 0.002 to 0.05
- power_limit: float32 [1024], P('net'), may hold values from 0.5 to 2
- store_node: int32 [1024], P('net'), may hold values from 0 to 4095, as said below
- line_factors: float32 [16, 512, 10, 256], P('net', 'scen'), may hold values from -0.125 to 0.125
- block_pattern: int32 [16, 10], P('net'), may hold values from 0 to 15, as said below
Outputs:
- next_generation: float32 [16, 168, 4096], P('scen', None, 'net')
- next_charging: float32 [16, 168, 1024], P('scen', None, 'net')
- next_discharging: float32 [16, 168, 1024], P('scen', None, 'net')
- next_plant: float32 [4096], P('net')
- next_store: float32 [1024], P('net')
- next_balance: float32 [16, 168], P('scen')
- next_line: float32 [16, 168, 8192], P('scen', None, 'net')
- next_headroom: float32 [16, 168, 4096], P('scen', None, 'net')
- next_empty: float32 [16, 168, 1024], P('scen', None, 'net')
- next_full: float32 [16, 168, 1024], P('scen', None, 'net')
The draws below stay inside these ranges and needn't reach their ends.
Inputs may be any that keep to these rules, and one draw needn't show every extreme that they name: `store_node`: storage unit k sits at a node of block k // 64. `block_pattern`: row b lists 10 different node blocks, the first of them b itself.
All inputs are finite; a program needn't handle non-finite values.
Results may differ from the reference program's by a relative error of at most 0.00016.
Values sent between devices are 32-bit elements; how exact they have to be, the bound alone decides.
A program may use at most 128 MiB of HBM per device.

```python
import math
import jax
import jax.numpy as jnp
from jax import lax

HOURS = 168
BLOCKS = 16
BLOCK = 256
BPAT = 10
GLINES = 512
STORE_BLK = 64
SCEN = 16
NODES = 4096
LINES = 8192
STORES = 1024


def draw_store_node(key, part):
    offsets = jax.random.randint(jax.random.fold_in(key, 7), (STORES,), 0, BLOCK)
    owners = jnp.arange(STORES, dtype=jnp.int32) // STORE_BLK
    placed = owners * BLOCK + offsets.astype(jnp.int32)
    placed = placed.at[0].set(0).at[STORES - 1].set(NODES - 1)
    return placed.astype(jnp.int32)


def draw_block_pattern(key, part):
    row_keys = jax.random.split(jax.random.fold_in(key, 11), BLOCKS)

    def one_row(row_key, own_block):
        ordering = jax.random.permutation(row_key, BLOCKS - 1)[:BPAT - 1].astype(jnp.int32)
        others = jnp.where(ordering >= own_block, ordering + 1, ordering)
        return jnp.concatenate([own_block[None], others]).astype(jnp.int32)
    return jax.vmap(one_row)(row_keys, jnp.arange(BLOCKS, dtype=jnp.int32))


def level_of(rng, extent, cuts, smallest, high):
    gain, own = 1.0, jax.random.fold_in(rng, 6)
    for position, parts in cuts:
        draws = jnp.exp(jax.random.uniform(jax.random.fold_in(own, position), (parts,), jnp.float32, smallest / len(cuts), high / len(cuts)))
        gain = gain * jnp.repeat(draws, extent[position] // parts).reshape([-1 if axis == position else 1 for axis in range(len(extent))])
    return gain


def gaussian(stream_key, extent, spread, limit, cuts=(), held_as=jnp.bfloat16):
    factor_of = level_of(stream_key, extent, cuts, -0.22, 0.18) if cuts else 1.0
    entries = jax.random.normal(stream_key, extent, jnp.float32) * spread * factor_of
    return jnp.minimum(jnp.maximum(entries, -limit), limit).astype(held_as)


def setup_inputs(seed: int = 0) -> dict:
    key_list = jax.random.split(jax.random.key(seed), 23)
    return {
        "generation": jnp.clip(2.0 * jax.random.uniform(key_list[0], (SCEN, HOURS, NODES), jnp.float32) ** level_of(key_list[0], (SCEN, HOURS, NODES), ((0, 16), (2, 2)), -0.2, 0.2), 0.0, 2.0),
        "charging": jnp.clip(0.5 * jax.random.uniform(key_list[1], (SCEN, HOURS, STORES), jnp.float32) ** level_of(key_list[1], (SCEN, HOURS, STORES), ((0, 16), (2, 2)), -0.2, 0.2), 0.0, 0.5),
        "discharging": jnp.clip(0.5 * jax.random.uniform(key_list[2], (SCEN, HOURS, STORES), jnp.float32) ** level_of(key_list[2], (SCEN, HOURS, STORES), ((0, 16), (2, 2)), -0.2, 0.2), 0.0, 0.5),
        "plant_capacity": jnp.clip(1.0 + 2.0 * jax.random.uniform(key_list[3], (NODES,), jnp.float32) ** level_of(key_list[3], (NODES,), ((0, 2),), -0.2, 0.2), 1.0, 3.0),
        "store_capacity": jnp.clip(4.0 + 8.0 * jax.random.uniform(key_list[4], (STORES,), jnp.float32) ** level_of(key_list[4], (STORES,), ((0, 2),), -0.2, 0.2), 4.0, 12.0),
        "dual_balance": gaussian(key_list[5], (SCEN, HOURS), 1.0, 6.0, ((0, 16),), jnp.float32),
        "dual_line": gaussian(key_list[6], (SCEN, HOURS, LINES), 1.0, 6.0, ((0, 16), (2, 2)), jnp.float32),
        "dual_headroom": jnp.clip(1.0 * jax.random.uniform(key_list[7], (SCEN, HOURS, NODES), jnp.float32) ** level_of(key_list[7], (SCEN, HOURS, NODES), ((0, 16), (2, 2)), -0.2, 0.2), 0.0, 1.0),
        "dual_empty": jnp.clip(-1.0 + 1.0 * jax.random.uniform(key_list[8], (SCEN, HOURS, STORES), jnp.float32) ** level_of(key_list[8], (SCEN, HOURS, STORES), ((0, 16), (2, 2)), -0.2, 0.2), -1.0, 0.0),
        "dual_full": jnp.clip(1.0 * jax.random.uniform(key_list[9], (SCEN, HOURS, STORES), jnp.float32) ** level_of(key_list[9], (SCEN, HOURS, STORES), ((0, 16), (2, 2)), -0.2, 0.2), 0.0, 1.0),
        "availability": jnp.clip(0.1 + 0.9 * jax.random.uniform(key_list[10], (SCEN, HOURS, NODES), jnp.float32) ** level_of(key_list[10], (SCEN, HOURS, NODES), ((0, 16), (2, 2)), -0.2, 0.2), 0.1, 1.0),
        "demand": jnp.clip(0.5 + 1.0 * jax.random.uniform(key_list[11], (SCEN, HOURS), jnp.float32) ** level_of(key_list[11], (SCEN, HOURS), ((0, 16),), -0.2, 0.2), 0.5, 1.5),
        "line_base": gaussian(key_list[12], (SCEN, HOURS, LINES), 1.0, 6.0, ((0, 16), (2, 2)), jnp.float32),
        "line_limit": jnp.clip(0.5 + 1.5 * jax.random.uniform(key_list[13], (LINES,), jnp.float32) ** level_of(key_list[13], (LINES,), ((0, 2),), -0.2, 0.2), 0.5, 2.0),
        "fuel_cost": jnp.clip(jnp.exp(math.log(2.0) - 2.9957323 * jax.random.uniform(key_list[14], (NODES,), jnp.float32) ** level_of(key_list[14], (NODES,), ((0, 2),), -0.2, 0.2)), 0.1, 2.0),
        "plant_cost": jnp.clip(jnp.exp(math.log(1.0) - 2.3025851 * jax.random.uniform(key_list[15], (NODES,), jnp.float32) ** level_of(key_list[15], (NODES,), ((0, 2),), -0.2, 0.2)), 0.1, 1.0),
        "store_cost": jnp.clip(jnp.exp(math.log(0.5) - 2.3025851 * jax.random.uniform(key_list[16], (STORES,), jnp.float32) ** level_of(key_list[16], (STORES,), ((0, 2),), -0.2, 0.2)), 0.05, 0.5),
        "self_loss": jnp.clip(jnp.exp(math.log(0.05) - 3.218876 * jax.random.uniform(key_list[17], (STORES,), jnp.float32) ** level_of(key_list[17], (STORES,), ((0, 2),), -0.2, 0.2)), 0.002, 0.05),
        "power_limit": jnp.clip(0.5 + 1.5 * jax.random.uniform(key_list[18], (STORES,), jnp.float32) ** level_of(key_list[18], (STORES,), ((0, 2),), -0.2, 0.2), 0.5, 2.0),
        "store_node": draw_store_node(jax.random.fold_in(key_list[22], 71), 0),
        "line_factors": gaussian(key_list[20], (BLOCKS, GLINES, BPAT, BLOCK), (BPAT * BLOCK) ** -0.5, 0.125, ((0, 2), (1, 16)), jnp.float32),
        "block_pattern": draw_block_pattern(jax.random.fold_in(key_list[22], 71), 0),
    }


highest = lax.Precision.HIGHEST
primal_step = 0.5
dual_step = 0.5
store_step = 0.05
level_step = 0.05
efficiency = 0.92


def line_dual_image(dual_line, line_factors, block_pattern):
    rows_all = SCEN * HOURS
    grouped_duals = dual_line.reshape(rows_all, BLOCKS, GLINES)

    def add_group(carry_image, group_index):
        factors = line_factors[group_index].reshape(GLINES, BPAT * BLOCK)
        line_duals = lax.dynamic_index_in_dim(grouped_duals, group_index, 1, keepdims=False)
        contribution = jnp.dot(line_duals, factors, precision=highest, preferred_element_type=jnp.float32)
        carry_image = carry_image.at[:, block_pattern[group_index], :].add(contribution.reshape(rows_all, BPAT, BLOCK))
        return carry_image, None

    initial = jnp.zeros((rows_all, BLOCKS, BLOCK), jnp.float32)
    nodal_image = lax.scan(add_group, initial, jnp.arange(BLOCKS, dtype=jnp.int32))[0]
    return nodal_image.reshape(SCEN, HOURS, NODES)


def flow_rows(injection, line_factors, block_pattern):
    rows_all = SCEN * HOURS
    blocks_all = injection.reshape(rows_all, BLOCKS, BLOCK)

    def one_group(group_index):
        chosen = blocks_all[:, block_pattern[group_index], :].reshape(rows_all, BPAT * BLOCK)
        factors = line_factors[group_index].reshape(GLINES, BPAT * BLOCK)
        return jnp.dot(chosen, factors.T, precision=highest, preferred_element_type=jnp.float32)

    outputs = lax.map(one_group, jnp.arange(BLOCKS, dtype=jnp.int32))
    return jnp.transpose(outputs, (1, 0, 2)).reshape(SCEN, HOURS, BLOCKS * GLINES)


def charge_levels(charge_drive, keep_rate):
    def advance(level_now, column):
        level_now = keep_rate * level_now + column
        return level_now, level_now

    initial = jnp.zeros((charge_drive.shape[0], charge_drive.shape[2]), jnp.float32)
    levels = lax.scan(advance, initial, jnp.transpose(charge_drive, (1, 0, 2)))[1]
    return jnp.transpose(levels, (1, 0, 2))


def charge_adjoint(weights, keep_rate):
    def retreat(level_now, column):
        level_now = keep_rate * level_now + column
        return level_now, level_now

    initial = jnp.zeros((weights.shape[0], weights.shape[2]), jnp.float32)
    levels = lax.scan(retreat, initial, jnp.transpose(weights, (1, 0, 2)), reverse=True)[1]
    return jnp.transpose(levels, (1, 0, 2))


def reference(generation, charging, discharging, plant_capacity, store_capacity, dual_balance, dual_line, dual_headroom, dual_empty, dual_full, availability, demand, line_base, line_limit, fuel_cost, plant_cost, store_cost, self_loss, power_limit, store_node, line_factors, block_pattern):
    keep_rate = 1.0 - self_loss
    line_image = line_dual_image(dual_line, line_factors, block_pattern)
    nodal_price = dual_balance[:, :, None] + line_image
    backward = charge_adjoint(dual_empty + dual_full, keep_rate)
    next_generation = jnp.maximum(generation - primal_step * (fuel_cost + nodal_price + dual_headroom), 0.0)
    store_price = nodal_price[:, :, store_node]
    next_charging = jnp.clip(charging - store_step * (efficiency * backward - store_price), 0.0, power_limit)
    next_discharging = jnp.clip(discharging - store_step * (store_price - backward / efficiency), 0.0, power_limit)
    plant_total = jnp.sum(availability * dual_headroom, axis=(0, 1))
    store_total = jnp.sum(dual_full, axis=(0, 1))
    next_plant = jnp.maximum(plant_capacity - primal_step * (plant_cost - plant_total / (SCEN * HOURS)), 0.0)
    next_store = jnp.maximum(store_capacity - primal_step * (store_cost - store_total / (SCEN * HOURS)), 0.0)
    extra_generation = 2.0 * next_generation - generation
    extra_charging = 2.0 * next_charging - charging
    extra_discharging = 2.0 * next_discharging - discharging
    extra_plant = 2.0 * next_plant - plant_capacity
    extra_store = 2.0 * next_store - store_capacity
    injection = extra_generation.at[:, :, store_node].add(extra_discharging - extra_charging)
    next_balance = dual_balance + dual_step * (jnp.sum(injection, axis=2) / NODES - demand)
    line_flows = flow_rows(injection, line_factors, block_pattern)
    line_moved = dual_line + dual_step * line_flows
    next_line = line_moved - dual_step * jnp.clip(line_moved / dual_step, -line_limit - line_base, line_limit - line_base)
    next_headroom = jnp.maximum(dual_headroom + dual_step * (extra_generation - availability * extra_plant), 0.0)
    levels = charge_levels(efficiency * extra_charging - extra_discharging / efficiency, keep_rate)
    next_empty = jnp.minimum(dual_empty + level_step * levels, 0.0)
    next_full = jnp.maximum(dual_full + level_step * (levels - extra_store), 0.0)
    return (next_generation, next_charging, next_discharging, next_plant, next_store, next_balance, next_line, next_headroom, next_empty, next_full)
```

```python
import functools

import jax
import jax.numpy as jnp
from jax import lax
from jax.experimental import pallas as pl
from jax.experimental.pallas import tpu as pltpu
from jax.sharding import PartitionSpec as P

LANES = 128
primal_step = 0.5
dual_step = 0.5
store_step = 0.05
level_step = 0.05
efficiency = 0.92
f32 = jnp.float32
bf16 = jnp.bfloat16
VMEM_BYTES = 56 * 1024 * 1024
MESH = pl.DeviceIdType.MESH
UP, DOWN, RIGHT, LEFT, CORE = range(5)


def split(x):
    hi = x.astype(bf16)
    return hi, (x - hi.astype(f32)).astype(bf16)


def stacked(x):
    return jnp.concatenate([x, x - x.astype(bf16).astype(f32)], axis=0).astype(bf16)


def dot(a, b):
    return jnp.dot(a, b, preferred_element_type=f32)


def dot_t(a, b):
    return lax.dot_general(a, b, (((1,), (1,)), ((), ())), preferred_element_type=f32)


def decayed_sums(x, keep, reverse):
    hours = x.shape[0]
    hour = lax.broadcasted_iota(jnp.int32, x.shape, 0)
    power = keep
    lag = 1
    while lag < hours:
        if reverse:
            moved = jnp.where(hour < hours - lag, pltpu.roll(x, hours - lag, 0), 0.0)
        else:
            moved = jnp.where(hour >= lag, pltpu.roll(x, lag, 0), 0.0)
        x = x + power * moved
        power = power * power
        lag *= 2
    return x


def when_all(conds, fn):
    if not conds:
        fn()
        return
    c = conds[0]
    for d in conds[1:]:
        c = jnp.logical_and(c, d)
    pl.when(c)(fn)


class Sizes:
    def __init__(self, scen, parts, generation, line_factors, store_node):
        _, self.hours, self.nodes = generation.shape
        self.groups, self.lines_local, self.slots, self.width = line_factors.shape
        self.scen, self.parts = scen, parts
        self.stores = store_node.shape[0]
        self.per = LANES // (self.stores // self.groups)
        assert self.per == 2
        self.cols = LANES // self.per
        self.chunks = self.width // self.cols
        self.pairs = -(-self.slots // self.per)
        self.wide = self.pairs * LANES
        self.lines = scen * self.lines_local
        self.rows = self.groups * self.lines_local
        self.blocks = self.groups * parts
        cut = -(-self.rows * 5 // 32 // 8) * 8
        self.cuts = ((0, self.rows - cut), (self.rows - cut, cut))
        plane = scen // 2
        self.rounds = scen.bit_length() - 1
        assert 2**self.rounds == scen
        self.b = max(d for d in range(1, plane + 1) if plane % d == 0 and d * d <= plane)
        self.a = plane // self.b


class Gather:
    def __init__(self, z, own, full, ssem, rsem):
        self.z, self.own, self.full, self.ssem, self.rsem = z, own, full, ssem, rsem
        self.me = lax.axis_index("scen")
        self.net = lax.axis_index("net")
        self.c = self.me % 2
        self.ib = (self.me // 2) % z.b
        self.ia = self.me // (2 * z.b)

    def slot(self, a, b):
        return (a * self.z.b + b) * 2 + self.c

    def has(self, way):
        return {
            UP: [self.ia < self.z.a - 1],
            DOWN: [self.ia > 0],
            RIGHT: [self.ib < self.z.b - 1],
            LEFT: [self.ib > 0],
            CORE: [],
        }[way]

    def device(self, way):
        z = self.z
        step = {UP: 2 * z.b, DOWN: -2 * z.b, RIGHT: 2, LEFT: -2}
        to = self.me + 1 - 2 * self.c if way == CORE else self.me + step[way]
        return (to, self.net)

    def copy(self, q, part, slot, way, own):
        start, size = self.z.cuts[part]
        rows = pl.ds(start, size)
        src = self.own.at[q, rows] if own else self.full.at[q, slot, rows]
        item = ((q * 2 + part) * (self.z.scen // 2) + slot // 2) * 5 + way
        return pltpu.make_async_remote_copy(
            src_ref=src,
            dst_ref=self.full.at[q, slot, rows],
            send_sem=self.ssem.at[item],
            recv_sem=self.rsem.at[(q * 2 + part) * self.z.scen + slot],
            device_id=self.device(way),
            device_id_type=MESH,
        )

    def arrivals(self):
        na, nb = self.z.a, self.z.b
        span = [0] + [s * k for k in range(1, na) for s in (-1, 1)]
        side = [0] + [s * k for k in range(1, nb) for s in (-1, 1)]
        steps = [[] for _ in range(na)]
        for t in range(na - 1):
            for s, way in ((-1, UP), (1, DOWN)):
                steps[t].append((0, s * (t + 1), 0, [way, RIGHT, LEFT, CORE]))
        for u in range(nb - 1):
            for s, way in ((-1, RIGHT), (1, LEFT)):
                steps[min(u, na - 1)].append((1, 0, s * (u + 1), [way, UP, DOWN, CORE]))
        for t in range(na - 1):
            for e in side:
                for s, way in ((-1, UP), (1, DOWN)):
                    steps[min(na - 1, t + max(abs(e) - 1, 0))].append((1, s * (t + 1), e, [way, CORE]))
        for u in range(nb - 1):
            for d in span:
                for s, way in ((-1, RIGHT), (1, LEFT)):
                    steps[min(na - 1, abs(d) + u)].append((0, d, s * (u + 1), [way, CORE]))
        return steps

    def valid(self, d, e):
        out = []
        if d < 0:
            out.append(self.ia + d >= 0)
        if d > 0:
            out.append(self.ia + d < self.z.a)
        if e < 0:
            out.append(self.ib + e >= 0)
        if e > 0:
            out.append(self.ib + e < self.z.b)
        return out

    def start_own(self, q):
        for part in range(2):
            for way in (UP, DOWN, RIGHT, LEFT, CORE):
                when_all(
                    self.has(way),
                    lambda: self.copy(q, part, self.me, way, True).start(),
                )

    def step(self, q, t):
        for part, d, e, ways in self.arrivals()[t]:
            def arrive(part=part, d=d, e=e, ways=ways):
                slot = self.slot(self.ia + d, self.ib + e)
                self.copy(q, part, slot, CORE, False).wait_recv()
                for way in ways:
                    when_all(
                        self.has(way),
                        lambda: self.copy(q, part, slot, way, False).start(),
                    )
            when_all(self.valid(d, e), arrive)

    def finish(self, q):
        def one(i, carry):
            for part in range(2):
                self.copy(q, part, 2 * i + 1 - self.c, CORE, False).wait_recv()
            return carry
        lax.fori_loop(0, self.z.scen // 2, one, 0)

    def drain(self, q):
        for part in range(2):
            for way in (UP, DOWN, RIGHT, LEFT, CORE):
                when_all(
                    self.has(way),
                    lambda: self.copy(q, part, self.me, way, True).wait_send(),
                )
        for step in self.arrivals():
            for part, d, e, ways in step:
                def sent(part=part, d=d, e=e, ways=ways):
                    slot = self.slot(self.ia + d, self.ib + e)
                    for way in ways:
                        when_all(
                            self.has(way),
                            lambda: self.copy(q, part, slot, way, False).wait_send(),
                        )
                when_all(self.valid(d, e), sent)


def step_kernel(
    z, pat, fac_h, line_h, base_h, gen_h, head_h, avail_h, chg_h, dis_h, empty_h, full_h,
    balance, demand, fuel, loss, power, node, limit, plant, plant_cost, stored, store_cost,
    full, gen_out, out_c, out_d, out_p, out_s, out_b, out_line, out_h, out_e, out_f,
    duals, wh, wl, fbuf, fac, own, parts_r, img, img_in, inj, inj_in, held,
    line, base, gen, head, avail, chg, dis, empty, dfull, back, price, place, total, sums, sums_in, tab,
    ssem, rsem, fsem, xsem, msem, tsem,
):
    me, net = lax.axis_index("scen"), lax.axis_index("net")
    half = z.groups // z.per
    lane = lax.broadcasted_iota(jnp.int32, (z.hours, LANES), 1)
    low = lane < z.cols
    ga = Gather(z, own, full, ssem, rsem)

    barrier = pltpu.get_barrier_semaphore()
    for way in (UP, DOWN, RIGHT, LEFT, CORE):
        when_all(
            ga.has(way),
            lambda: pl.semaphore_signal(
                barrier, inc=1, device_id=ga.device(way), device_id_type=MESH
            ),
        )
    for s in range(1, z.parts):
        pl.semaphore_signal(
            barrier, inc=1, device_id=(me, (net + s) % z.parts), device_id_type=MESH
        )

    def mate(r):
        bit = 2**r
        return (me + bit - 2 * bit * ((me // bit) % 2), net)

    for r in range(z.rounds):
        pl.semaphore_signal(barrier, inc=1, device_id=mate(r), device_id_type=MESH)
    met = jnp.int32(z.parts + z.rounds)
    for way in (UP, DOWN, RIGHT, LEFT):
        for c in ga.has(way):
            met = met + c.astype(jnp.int32)

    loads = [
        pltpu.make_async_copy(h, v, msem.at[i])
        for i, (h, v) in enumerate(
            [
                (fac_h, fac), (line_h, line), (empty_h, empty), (full_h, dfull), (head_h, head),
                (avail_h, avail), (gen_h, gen), (chg_h, chg), (dis_h, dis), (base_h, base),
            ]
        )
    ]
    for c in loads:
        c.start()

    def own_copy(q):
        return pltpu.make_async_copy(own.at[q], full.at[q, me], msem.at[len(loads) + q])

    def lay_out(q):
        even = q % 2 == 0
        tile = pl.ds(pl.multiple_of((q // 2) * LANES, LANES), LANES)
        here = lax.broadcasted_iota(jnp.int32, (z.lines_local, LANES), 1) < z.cols
        for g in range(z.groups):
            for p in range(z.pairs):
                x = fac[g, 2 * p, :, tile]
                y = fac[g, 2 * p + 1, :, tile] if 2 * p + 1 < z.slots else jnp.zeros_like(x)
                keep = jnp.where(even, x, y)
                turn = pltpu.roll(jnp.where(even, y, x), z.cols, 1)
                own[q, g * z.lines_local : (g + 1) * z.lines_local, p * LANES : (p + 1) * LANES] = (
                    jnp.where(here == even, keep, turn)
                )

    def begin(q):
        lay_out(q)
        ga.start_own(q)
        own_copy(q).start()

    def sum_copy(r):
        return pltpu.make_async_remote_copy(
            src_ref=sums.at[r],
            dst_ref=sums_in.at[r],
            send_sem=tsem.at[r],
            recv_sem=tsem.at[z.rounds + r],
            device_id=mate(r),
            device_id_type=MESH,
        )

    loads[0].wait()
    lay_out(0)
    pl.semaphore_wait(barrier, met)
    ga.start_own(0)
    own_copy(0).start()

    for c in loads[1:4]:
        c.wait()

    def take_line(g, carry):
        cols = pl.ds(pl.multiple_of(g * z.lines, z.lines), z.lines)
        duals[g] = stacked(line[:, cols])
        parts_r[g * (z.pairs + 1) + z.pairs] = jnp.zeros((z.hours, LANES), f32)
        return carry

    lax.fori_loop(0, z.groups, take_line, 0)

    def find(m, carry):
        def in_group(g, carry):
            for k in range(2):
                found = jnp.int32(z.pairs)
                for p in range(z.pairs):
                    j = 2 * p + k
                    if j < z.slots:
                        block = lax.rem(pat[g, j] - net * z.groups + z.blocks, z.blocks)
                        found = jnp.where(block == m, p, found)
                tab[(k * z.blocks + m) * z.groups + g] = g * (z.pairs + 1) + found
            return carry

        return lax.fori_loop(0, z.groups, in_group, carry)

    lax.fori_loop(0, z.blocks, find, 0)

    at = (node[...] - net * z.nodes).astype(f32)
    block = jnp.floor((at + 0.5) / z.width)
    col = at - block * z.width
    unit = lax.broadcasted_iota(jnp.int32, at.shape, 1).astype(f32)
    pair_of = jnp.floor((unit + 0.5) / LANES)
    part_of = jnp.floor((col + 0.5) / z.cols)
    spot = (block - pair_of * z.per) * z.cols + col - part_of * z.cols
    for q in range(z.chunks):
        place[q] = jnp.where(part_of == q, spot, -1.0)

    back[...] = decayed_sums(empty[...] + dfull[...], 1.0 - loss[...], True)
    price[...] = jnp.zeros_like(price)
    out_line[...] = jnp.zeros_like(out_line)
    total[...] = jnp.zeros_like(total)
    for c in loads[4:]:
        c.wait()
    sums[0, :, : z.nodes] = jnp.sum(avail[...] * head[...], axis=0, keepdims=True)
    sums[0, :, z.nodes :] = jnp.sum(dfull[...], axis=0, keepdims=True)
    sum_copy(0).start()

    hour_r = lax.broadcasted_iota(jnp.int32, (z.hours, z.hours), 0)
    hour_c = lax.broadcasted_iota(jnp.int32, (z.hours, z.hours), 1)
    eye = hour_r == hour_c
    balance_col = jnp.sum(jnp.where(eye, balance[...], 0.0), axis=1, keepdims=True)

    def factor_copy(q, g):
        return pltpu.make_async_copy(
            full.at[q, :, pl.ds(pl.multiple_of(g * z.lines_local, 8), z.lines_local)],
            fbuf.at[g % 2], fsem.at[g % 2],
        )

    def image(q):
        factor_copy(q, 0).start()

        def group(g, carry):
            factor_copy(q, g).wait()

            @pl.when(g + 1 < z.groups)
            def _():
                factor_copy(q, g + 1).start()

            for c0 in range(0, z.wide, 2 * LANES):
                c1 = min(c0 + 2 * LANES, z.wide)
                w = fbuf[g % 2, :, :, c0:c1].reshape(z.lines, c1 - c0)
                hi, lo = split(w)
                wh[g, :, c0:c1] = hi
                wl[g, :, c0:c1] = lo
                r = dot(duals[g], hi)
                r = r[: z.hours] + r[z.hours :] + dot(duals[g, : z.hours], lo)
                for p in range(c0 // LANES, c1 // LANES):
                    parts_r[g * (z.pairs + 1) + p] = r[:, p * LANES - c0 : (p + 1) * LANES - c0]
            return carry

        lax.fori_loop(0, z.groups, group, 0)

    def collect(first, last):
        def pair(m, carry):
            found = []
            for k in range(2):
                for i in range(2):
                    x = jnp.zeros((z.hours, LANES), f32)
                    for g in range(z.groups):
                        x = x + parts_r[tab[(k * z.blocks + m * 2 + i) * z.groups + g]]
                    found.append(x)
            low0, low1, high0, high1 = found
            crossed = jnp.where(low, low1, high0)
            img[m] = jnp.where(low, low0, high1) + pltpu.roll(crossed, z.cols, 1)
            return carry

        lax.fori_loop(first, last, pair, 0)

    def img_copy(s):
        return pltpu.make_async_remote_copy(
            src_ref=img.at[pl.ds(s * half, half)],
            dst_ref=img_in.at[pl.ds((s - 1) * half, half)],
            send_sem=xsem.at[s - 1],
            recv_sem=xsem.at[z.parts - 1 + s - 1],
            device_id=(me, (net + s) % z.parts),
            device_id_type=MESH,
        )

    def inj_copy(s):
        return pltpu.make_async_remote_copy(
            src_ref=inj,
            dst_ref=inj_in.at[pl.ds((s - 1) * half, half)],
            send_sem=xsem.at[2 * (z.parts - 1) + s - 1],
            recv_sem=xsem.at[3 * (z.parts - 1) + s - 1],
            device_id=(me, (net - s + z.parts) % z.parts),
            device_id_type=MESH,
        )

    def hold(m, x):
        turned = pltpu.roll(x, z.cols, 1)
        zero = jnp.zeros_like(x)
        held[0, 2 * m] = stacked(jnp.where(low, x, zero))
        held[1, 2 * m] = stacked(jnp.where(low, zero, turned))
        held[0, 2 * m + 1] = stacked(jnp.where(low, turned, zero))
        held[1, 2 * m + 1] = stacked(jnp.where(low, zero, x))

    def dispatch(q):
        even = q % 2 == 0
        tile = (q // 2) * LANES

        def packed(ref, t):
            x = ref[:, pl.ds(pl.multiple_of((2 * t) * z.width + tile, LANES), LANES)]
            y = ref[:, pl.ds(pl.multiple_of((2 * t + 1) * z.width + tile, LANES), LANES)]
            here = lax.broadcasted_iota(jnp.int32, x.shape, 1) < z.cols
            keep = jnp.where(even, x, y)
            turn = pltpu.roll(jnp.where(even, y, x), z.cols, 1)
            return jnp.where(here == even, keep, turn)

        def pair(t, carry):
            image_t = img[t]
            for s in range(1, z.parts):
                image_t = image_t + img_in[(s - 1) * half + t]
            price_t = balance_col + image_t
            gen_t = packed(gen, t)
            moved = jnp.maximum(
                gen_t - primal_step * (packed(fuel, t) + price_t + packed(head, t)), 0.0
            )
            turned = pltpu.roll(moved, z.cols, 1)
            for i in range(2):
                cols = pl.ds(pl.multiple_of((2 * t + i) * z.width + tile, LANES), LANES)
                mine = jnp.where(even, moved if i == 0 else turned, turned if i == 0 else moved)
                gen_out[:, cols] = jnp.where(low == even, mine, gen_out[:, cols])
            units = pl.ds(pl.multiple_of(t * LANES, LANES), LANES)
            row = lax.broadcasted_iota(jnp.int32, (LANES, LANES), 0).astype(f32)
            marks = jnp.where(row == place[q, :, units], 1.0, 0.0).astype(bf16)
            hi, lo = split(price_t)
            cost = price[:, units] + (dot(hi, marks) + dot(lo, marks))
            price[:, units] = cost
            b = back[:, units]
            cap = power[:, units]
            c, d = chg[:, units], dis[:, units]
            next_c = jnp.minimum(jnp.maximum(c - store_step * (efficiency * b - cost), 0.0), cap)
            next_d = jnp.minimum(jnp.maximum(d - store_step * (cost - b / efficiency), 0.0), cap)
            out_c[:, units] = next_c
            out_d[:, units] = next_d
            hi, lo = split((2.0 * next_d - d) - (2.0 * next_c - c))
            inj[t] = (2.0 * moved - gen_t) + (dot_t(hi, marks) + dot_t(lo, marks))
            return carry

        lax.fori_loop(0, half, pair, 0)

    def hold_own(t, carry):
        x = inj[t]
        total[...] += x
        hold(t, x)
        return carry

    def hold_in(t, carry):
        x = inj_in[t]
        total[...] += x
        hold(half + t, x)
        return carry

    def flow(g, carry):
        cols = pl.ds(pl.multiple_of(g * z.lines, z.lines), z.lines)
        both = []
        for p in range(z.pairs):
            x = None
            for k in range(2):
                if 2 * p + k < z.slots:
                    m = lax.rem(pat[g, 2 * p + k] - net * z.groups + z.blocks, z.blocks)
                    y = held[k, m]
                    x = y if x is None else x + y
            both.append(x)
        both = jnp.concatenate(both, axis=1)
        r = dot_t(both, wh[g])
        r = r[: z.hours] + r[z.hours :] + dot_t(both[: z.hours], wl[g])
        out_line[:, cols] = out_line[:, cols] + r
        return carry

    steps = z.a
    lag = 2
    ready = -(-(steps + 2) // lag)

    def events(k, keep):
        found = []
        for o in range(lag):
            for t in range(steps, -1, -1):
                if (t - o) % lag == 0 and keep(t):
                    found.append((o, t, k - (t - o) // lag))
        last = steps + 1
        if keep(last):
            found.append((last % lag, last, k - last // lag))
        for _, t, q in found:
            live = jnp.logical_and(q >= 0, q < z.chunks)

            def act(t=t, q=q):
                if t == 0:
                    pl.when(q > 0)(lambda: begin(q))
                elif t <= steps:
                    ga.step(q, t - 1)
                else:
                    ga.finish(q)
                    own_copy(q).wait()

            pl.when(live)(act)

    def beat(k, carry):
        q = k - ready
        live = jnp.logical_and(q >= 0, q < z.chunks)

        for r in range(1, z.rounds + 1):
            @pl.when(k == r)
            def _():
                sum_copy(r - 1).wait_recv()
                sums[r] = sums[r - 1] + sums_in[r - 1]
                if r < z.rounds:
                    sum_copy(r).start()

        events(k, lambda t: t == 0)

        @pl.when(live)
        def _():
            image(q)

            @pl.when(q > 0)
            def _():
                for s in range(1, z.parts):
                    img_copy(s).wait_send()
                    inj_copy(s).wait_send()

            for s in range(1, z.parts):
                collect(s * half, (s + 1) * half)
                img_copy(s).start()
            collect(0, half)

        events(k, lambda t: 0 < t < steps and t % lag == 0)

        @pl.when(live)
        def _():
            for s in range(1, z.parts):
                img_copy(s).wait_recv()
            dispatch(q)
            for s in range(1, z.parts):
                inj_copy(s).start()
            lax.fori_loop(0, half, hold_own, 0)
            for s in range(1, z.parts):
                inj_copy(s).wait_recv()
            lax.fori_loop(0, half * (z.parts - 1), hold_in, 0)
            lax.fori_loop(0, z.groups, flow, 0)

        events(k, lambda t: t >= steps or t % lag)
        return carry

    lax.fori_loop(0, z.chunks + ready, beat, 0)

    for s in range(1, z.parts):
        img_copy(s).wait_send()
        inj_copy(s).wait_send()

    for g in range(z.groups):
        cols = slice(g * z.lines, (g + 1) * z.lines)
        moved = line[:, cols] + dual_step * out_line[:, cols]
        floor = -limit[:, cols] - base[:, cols]
        ceiling = limit[:, cols] - base[:, cols]
        out_line[:, cols] = moved - dual_step * jnp.minimum(
            jnp.maximum(moved / dual_step, floor), ceiling
        )
    found = sums[z.rounds]
    next_plant = jnp.maximum(
        plant[...] - primal_step * (plant_cost[...] - found[:, : z.nodes] / (z.scen * z.hours)), 0.0
    )
    next_store = jnp.maximum(
        stored[...] - primal_step * (store_cost[...] - found[:, z.nodes :] / (z.scen * z.hours)), 0.0
    )
    out_p[...] = next_plant
    out_s[...] = next_store
    extra_plant = 2.0 * next_plant - plant[...]
    extra_store = 2.0 * next_store - stored[...]
    out_h[...] = jnp.maximum(
        head[...] + dual_step * ((2.0 * gen_out[...] - gen[...]) - avail[...] * extra_plant), 0.0
    )
    extra_c = 2.0 * out_c[...] - chg[...]
    extra_d = 2.0 * out_d[...] - dis[...]
    levels = decayed_sums(efficiency * extra_c - extra_d / efficiency, 1.0 - loss[...], False)
    out_e[...] = jnp.minimum(empty[...] + level_step * levels, 0.0)
    out_f[...] = jnp.maximum(dfull[...] + level_step * (levels - extra_store), 0.0)
    col_total = jnp.sum(total[...], axis=1, keepdims=True)
    row_total = jnp.sum(jnp.where(eye, col_total, 0.0), axis=0, keepdims=True)
    out_b[...] = balance[...] + dual_step * (row_total / (z.blocks * z.width) - demand[...])

    for r in range(z.rounds):
        sum_copy(r).wait_send()

    def drained(q, carry):
        ga.drain(q)
        return carry

    lax.fori_loop(0, z.chunks, drained, 0)


def run_step(z, pat, big, small):
    h, n, st, ln = z.hours, z.nodes, z.stores, z.groups * z.lines
    half = z.groups // z.per
    others = z.parts - 1
    hbm = pl.BlockSpec(memory_space=pltpu.HBM)
    vmem = pl.BlockSpec(memory_space=pltpu.VMEM)
    smem = pl.BlockSpec(memory_space=pltpu.SMEM)

    def shape(*dims):
        return jax.ShapeDtypeStruct(dims, f32)

    def buffer(*dims, dtype=f32):
        return pltpu.VMEM(dims, dtype)

    outs = [
        shape(z.chunks, z.scen, z.rows, z.wide), shape(h, n), shape(h, st), shape(h, st),
        shape(1, n), shape(1, st), shape(1, h), shape(h, ln), shape(h, n), shape(h, st), shape(h, st),
    ]
    return pl.pallas_call(
        functools.partial(step_kernel, z),
        out_shape=outs,
        in_specs=[smem] + [hbm] * len(big) + [vmem] * len(small),
        out_specs=[hbm] + [vmem] * (len(outs) - 1),
        scratch_shapes=[
            buffer(z.groups, 2 * h, z.lines, dtype=bf16),
            buffer(z.groups, z.lines, z.wide, dtype=bf16),
            buffer(z.groups, z.lines, z.wide, dtype=bf16),
            buffer(2, z.scen, z.lines_local, z.wide),
            buffer(z.groups, z.slots, z.lines_local, z.width),
            buffer(z.chunks, z.rows, z.wide),
            buffer(z.groups * (z.pairs + 1), h, LANES),
            buffer(z.parts * half, h, LANES),
            buffer(others * half, h, LANES),
            buffer(half, h, LANES),
            buffer(others * half, h, LANES),
            buffer(2, z.blocks, 2 * h, LANES, dtype=bf16),
            buffer(h, ln),
            buffer(h, ln),
        ]
        + [buffer(h, n)] * 3
        + [buffer(h, st)] * 6
        + [
            buffer(z.chunks, 1, st),
            buffer(h, LANES),
            buffer(z.rounds + 1, 1, n + st),
            buffer(z.rounds, 1, n + st),
            pltpu.SMEM((2 * z.blocks * z.groups,), jnp.int32),
            pltpu.SemaphoreType.DMA((z.chunks * 2 * (z.scen // 2) * 5,)),
            pltpu.SemaphoreType.DMA((z.chunks * 2 * z.scen,)),
            pltpu.SemaphoreType.DMA((2,)),
            pltpu.SemaphoreType.DMA((4 * others,)),
            pltpu.SemaphoreType.DMA((len(big) + z.chunks,)),
            pltpu.SemaphoreType.DMA((2 * z.rounds,)),
        ],
        compiler_params=pltpu.CompilerParams(
            vmem_limit_bytes=VMEM_BYTES, collective_id=0, has_side_effects=True
        ),
        cost_estimate=pl.CostEstimate(
            flops=12 * h * z.groups * z.lines * z.slots * z.width,
            bytes_accessed=12 * z.groups * z.lines * z.slots * z.width,
            transcendentals=0,
        ),
        name="iteration",
    )(pat, *big, *small)


def body(
    generation, charging, discharging, plant_capacity, store_capacity, dual_balance, dual_line,
    dual_headroom, dual_empty, dual_full, availability, demand, line_base, line_limit, fuel_cost,
    plant_cost, store_cost, self_loss, power_limit, store_node, line_factors, block_pattern,
):
    z = Sizes(lax.axis_size("scen"), lax.axis_size("net"), generation, line_factors, store_node)
    big = [
        line_factors.transpose(0, 2, 1, 3), dual_line[0], line_base[0], generation[0],
        dual_headroom[0], availability[0], charging[0], discharging[0], dual_empty[0], dual_full[0],
    ]
    small = [dual_balance, demand] + [
        x[None]
        for x in (
            fuel_cost, self_loss, power_limit, store_node, line_limit,
            plant_capacity, plant_cost, store_capacity, store_cost,
        )
    ]
    outs = run_step(z, block_pattern, big, small)
    gen, chg, dis, plant, stored, balance, line, head, empty, full = outs[1:]
    return (
        gen[None], chg[None], dis[None], plant[0], stored[0], balance,
        line[None], head[None], empty[None], full[None],
    )


def solution(mesh):
    row = P("scen", None, "net")
    placed = (
        row, row, row, P("net"), P("net"), P("scen", None), row, row, row, row, row,
        P("scen", None), row, P("net"), P("net"), P("net"), P("net"), P("net"), P("net"), P("net"),
        P("net", "scen", None, None), P("net", None),
    )
    return jax.shard_map(
        body,
        mesh=mesh,
        in_specs=placed,
        out_specs=(row, row, row, P("net"), P("net"), P("scen", None), row, row, row, row),
        check_vma=False,
    )
```

```python
import functools

import jax
import jax.numpy as jnp
from jax import lax
from jax.experimental import pallas as pl
from jax.experimental.pallas import tpu as pltpu
from jax.sharding import PartitionSpec as P

LANES = 128
primal_step = 0.5
dual_step = 0.5
store_step = 0.05
level_step = 0.05
efficiency = 0.92
f32 = jnp.float32
bf16 = jnp.bfloat16
VMEM_BYTES = 56 * 1024 * 1024
MESH = pl.DeviceIdType.MESH
UP, DOWN, RIGHT, LEFT, CORE = range(5)


def split(x):
    hi = x.astype(bf16)
    return hi, (x - hi.astype(f32)).astype(bf16)


def stacked(x):
    return jnp.concatenate([x, x - x.astype(bf16).astype(f32)], axis=0).astype(bf16)


def dot(a, b):
    return jnp.dot(a, b, preferred_element_type=f32)


def dot_t(a, b):
    return lax.dot_general(a, b, (((1,), (1,)), ((), ())), preferred_element_type=f32)


def decayed_sums(x, keep, reverse):
    hours = x.shape[0]
    hour = lax.broadcasted_iota(jnp.int32, x.shape, 0)
    power = keep
    lag = 1
    while lag < hours:
        if reverse:
            moved = jnp.where(hour < hours - lag, pltpu.roll(x, hours - lag, 0), 0.0)
        else:
            moved = jnp.where(hour >= lag, pltpu.roll(x, lag, 0), 0.0)
        x = x + power * moved
        power = power * power
        lag *= 2
    return x


def when_all(conds, fn):
    if not conds:
        fn()
        return
    c = conds[0]
    for d in conds[1:]:
        c = jnp.logical_and(c, d)
    pl.when(c)(fn)


class Sizes:
    def __init__(self, scen, parts, generation, line_factors, store_node):
        _, self.hours, self.nodes = generation.shape
        self.groups, self.lines_local, self.slots, self.width = line_factors.shape
        self.scen, self.parts = scen, parts
        self.stores = store_node.shape[0]
        self.per = LANES // (self.stores // self.groups)
        assert self.per == 2
        self.cols = LANES // self.per
        self.chunks = self.width // self.cols
        self.pairs = -(-self.slots // self.per)
        self.wide = self.pairs * LANES
        self.lines = scen * self.lines_local
        self.rows = self.groups * self.lines_local
        self.blocks = self.groups * parts
        cut = -(-self.rows * 5 // 32 // 8) * 8
        self.cuts = ((0, self.rows - cut), (self.rows - cut, cut))
        plane = scen // 2
        self.rounds = scen.bit_length() - 1
        assert 2**self.rounds == scen
        self.b = max(d for d in range(1, plane + 1) if plane % d == 0 and d * d <= plane)
        self.a = plane // self.b


class Gather:
    def __init__(self, z, own, full, ssem, rsem):
        self.z, self.own, self.full, self.ssem, self.rsem = z, own, full, ssem, rsem
        self.me = lax.axis_index("scen")
        self.net = lax.axis_index("net")
        self.c = self.me % 2
        self.ib = (self.me // 2) % z.b
        self.ia = self.me // (2 * z.b)

    def slot(self, a, b):
        return (a * self.z.b + b) * 2 + self.c

    def has(self, way):
        return {
            UP: [self.ia < self.z.a - 1],
            DOWN: [self.ia > 0],
            RIGHT: [self.ib < self.z.b - 1],
            LEFT: [self.ib > 0],
            CORE: [],
        }[way]

    def device(self, way):
        z = self.z
        step = {UP: 2 * z.b, DOWN: -2 * z.b, RIGHT: 2, LEFT: -2}
        to = self.me + 1 - 2 * self.c if way == CORE else self.me + step[way]
        return (to, self.net)

    def copy(self, q, part, slot, way, own):
        start, size = self.z.cuts[part]
        rows = pl.ds(start, size)
        src = self.own.at[q, rows] if own else self.full.at[q, slot, rows]
        item = ((q * 2 + part) * (self.z.scen // 2) + slot // 2) * 5 + way
        return pltpu.make_async_remote_copy(
            src_ref=src,
            dst_ref=self.full.at[q, slot, rows],
            send_sem=self.ssem.at[item],
            recv_sem=self.rsem.at[(q * 2 + part) * self.z.scen + slot],
            device_id=self.device(way),
            device_id_type=MESH,
        )

    def arrivals(self):
        na, nb = self.z.a, self.z.b
        span = [0] + [s * k for k in range(1, na) for s in (-1, 1)]
        side = [0] + [s * k for k in range(1, nb) for s in (-1, 1)]
        steps = [[] for _ in range(na)]
        for t in range(na - 1):
            for s, way in ((-1, UP), (1, DOWN)):
                steps[t].append((0, s * (t + 1), 0, [way, RIGHT, LEFT, CORE]))
        for u in range(nb - 1):
            for s, way in ((-1, RIGHT), (1, LEFT)):
                steps[min(u, na - 1)].append((1, 0, s * (u + 1), [way, UP, DOWN, CORE]))
        for t in range(na - 1):
            for e in side:
                for s, way in ((-1, UP), (1, DOWN)):
                    steps[min(na - 1, t + max(abs(e) - 1, 0))].append((1, s * (t + 1), e, [way, CORE]))
        for u in range(nb - 1):
            for d in span:
                for s, way in ((-1, RIGHT), (1, LEFT)):
                    steps[min(na - 1, abs(d) + u)].append((0, d, s * (u + 1), [way, CORE]))
        return steps

    def valid(self, d, e):
        out = []
        if d < 0:
            out.append(self.ia + d >= 0)
        if d > 0:
            out.append(self.ia + d < self.z.a)
        if e < 0:
            out.append(self.ib + e >= 0)
        if e > 0:
            out.append(self.ib + e < self.z.b)
        return out

    def start_own(self, q):
        for part in range(2):
            for way in (UP, DOWN, RIGHT, LEFT, CORE):
                when_all(
                    self.has(way),
                    lambda: self.copy(q, part, self.me, way, True).start(),
                )

    def step(self, q, t):
        for part, d, e, ways in self.arrivals()[t]:
            def arrive(part=part, d=d, e=e, ways=ways):
                slot = self.slot(self.ia + d, self.ib + e)
                self.copy(q, part, slot, CORE, False).wait_recv()
                for way in ways:
                    when_all(
                        self.has(way),
                        lambda: self.copy(q, part, slot, way, False).start(),
                    )
            when_all(self.valid(d, e), arrive)

    def finish(self, q):
        def one(i, carry):
            for part in range(2):
                self.copy(q, part, 2 * i + 1 - self.c, CORE, False).wait_recv()
            return carry
        lax.fori_loop(0, self.z.scen // 2, one, 0)

    def drain(self, q):
        for part in range(2):
            for way in (UP, DOWN, RIGHT, LEFT, CORE):
                when_all(
                    self.has(way),
                    lambda: self.copy(q, part, self.me, way, True).wait_send(),
                )
        for step in self.arrivals():
            for part, d, e, ways in step:
                def sent(part=part, d=d, e=e, ways=ways):
                    slot = self.slot(self.ia + d, self.ib + e)
                    for way in ways:
                        when_all(
                            self.has(way),
                            lambda: self.copy(q, part, slot, way, False).wait_send(),
                        )
                when_all(self.valid(d, e), sent)


def step_kernel(
    z, pat, fac_h, line_h, base_h, gen_h, head_h, avail_h, chg_h, dis_h, empty_h, full_h,
    balance, demand, fuel, loss, power, node, limit, plant, plant_cost, stored, store_cost,
    full, out_gen, out_c, out_d, out_p, out_s, out_line, out_h, out_e, out_f, out_b,
    duals, wh, wl, fbuf, fac, own, parts_r, img, img_in, inj, inj_in, held,
    line, base, gen, head, avail, chg, dis, empty, dfull, back, price, next_c, next_d, next_e, next_f,
    place, total, sums, sums_in, acc, next_gen, next_h, next_p, next_s, level, tab,
    ssem, rsem, fsem, xsem, msem, tsem, osem,
):
    me, net = lax.axis_index("scen"), lax.axis_index("net")
    half = z.groups // z.per
    lane = lax.broadcasted_iota(jnp.int32, (z.hours, LANES), 1)
    low = lane < z.cols
    ga = Gather(z, own, full, ssem, rsem)

    barrier = pltpu.get_barrier_semaphore()
    for way in (UP, DOWN, RIGHT, LEFT, CORE):
        when_all(
            ga.has(way),
            lambda: pl.semaphore_signal(
                barrier, inc=1, device_id=ga.device(way), device_id_type=MESH
            ),
        )
    for s in range(1, z.parts):
        pl.semaphore_signal(
            barrier, inc=1, device_id=(me, (net + s) % z.parts), device_id_type=MESH
        )

    def mate(r):
        bit = 2**r
        return (me + bit - 2 * bit * ((me // bit) % 2), net)

    for r in range(z.rounds):
        pl.semaphore_signal(barrier, inc=1, device_id=mate(r), device_id_type=MESH)
    met = jnp.int32(z.parts + z.rounds)
    for way in (UP, DOWN, RIGHT, LEFT):
        for c in ga.has(way):
            met = met + c.astype(jnp.int32)

    loads = [
        pltpu.make_async_copy(h, v, msem.at[i])
        for i, (h, v) in enumerate(
            [
                (fac_h, fac), (line_h, line), (empty_h, empty), (full_h, dfull), (head_h, head),
                (avail_h, avail), (gen_h, gen), (chg_h, chg), (dis_h, dis), (base_h, base),
            ]
        )
    ]
    for c in loads:
        c.start()

    def own_copy(q):
        return pltpu.make_async_copy(own.at[q], full.at[q, me], msem.at[len(loads) + q])

    def lay_out(q):
        even = q % 2 == 0
        tile = pl.ds(pl.multiple_of((q // 2) * LANES, LANES), LANES)
        here = lax.broadcasted_iota(jnp.int32, (z.lines_local, LANES), 1) < z.cols
        for g in range(z.groups):
            for p in range(z.pairs):
                x = fac[g, 2 * p, :, tile]
                y = fac[g, 2 * p + 1, :, tile] if 2 * p + 1 < z.slots else jnp.zeros_like(x)
                keep = jnp.where(even, x, y)
                turn = pltpu.roll(jnp.where(even, y, x), z.cols, 1)
                own[q, g * z.lines_local : (g + 1) * z.lines_local, p * LANES : (p + 1) * LANES] = (
                    jnp.where(here == even, keep, turn)
                )

    def begin(q):
        lay_out(q)
        ga.start_own(q)
        own_copy(q).start()

    def sum_copy(r):
        return pltpu.make_async_remote_copy(
            src_ref=sums.at[r],
            dst_ref=sums_in.at[r],
            send_sem=tsem.at[r],
            recv_sem=tsem.at[z.rounds + r],
            device_id=mate(r),
            device_id_type=MESH,
        )

    loads[0].wait()
    lay_out(0)
    pl.semaphore_wait(barrier, met)
    ga.start_own(0)
    own_copy(0).start()

    hour_r = lax.broadcasted_iota(jnp.int32, (z.hours, z.hours), 0)
    hour_c = lax.broadcasted_iota(jnp.int32, (z.hours, z.hours), 1)
    eye = hour_r == hour_c

    def take_line(g, carry):
        cols = pl.ds(pl.multiple_of(g * z.lines, z.lines), z.lines)
        duals[g] = stacked(line[:, cols])
        parts_r[g * (z.pairs + 1) + z.pairs] = jnp.zeros((z.hours, LANES), f32)
        return carry

    def find(m, carry):
        def in_group(g, carry):
            for k in range(2):
                found = jnp.int32(z.pairs)
                for p in range(z.pairs):
                    j = 2 * p + k
                    if j < z.slots:
                        block = lax.rem(pat[g, j] - net * z.groups + z.blocks, z.blocks)
                        found = jnp.where(block == m, p, found)
                tab[(k * z.blocks + m) * z.groups + g] = g * (z.pairs + 1) + found
            return carry

        return lax.fori_loop(0, z.groups, in_group, carry)

    def prepare_sums():
        for c in loads[1:]:
            c.wait()
        sums[0, :, : z.nodes] = jnp.sum(avail[...] * head[...], axis=0, keepdims=True)
        sums[0, :, z.nodes :] = jnp.sum(dfull[...], axis=0, keepdims=True)
        sum_copy(0).start()
        price[...] = jnp.zeros_like(price)
        total[...] = jnp.zeros_like(total)
        acc[...] = jnp.zeros_like(acc)
        lax.fori_loop(0, z.groups, take_line, 0)

    def prepare_tables():
        lax.fori_loop(0, z.blocks, find, 0)
        at = (node[...] - net * z.nodes).astype(f32)
        block = jnp.floor((at + 0.5) / z.width)
        col = at - block * z.width
        unit = lax.broadcasted_iota(jnp.int32, at.shape, 1).astype(f32)
        pair_of = jnp.floor((unit + 0.5) / LANES)
        part_of = jnp.floor((col + 0.5) / z.cols)
        spot = (block - pair_of * z.per) * z.cols + col - part_of * z.cols
        for q in range(z.chunks):
            place[q] = jnp.where(part_of == q, spot, -1.0)
        back[...] = decayed_sums(empty[...] + dfull[...], 1.0 - loss[...], True)
        column = jnp.sum(jnp.where(eye, balance[...], 0.0), axis=1, keepdims=True)
        level[...] = jnp.broadcast_to(column, level.shape)

    def factor_copy(q, g):
        return pltpu.make_async_copy(
            full.at[q, :, pl.ds(pl.multiple_of(g * z.lines_local, 8), z.lines_local)],
            fbuf.at[g % 2], fsem.at[g % 2],
        )

    def image(q):
        factor_copy(q, 0).start()

        def group(g, carry):
            factor_copy(q, g).wait()

            @pl.when(g + 1 < z.groups)
            def _():
                factor_copy(q, g + 1).start()

            for c0 in range(0, z.wide, 2 * LANES):
                c1 = min(c0 + 2 * LANES, z.wide)
                w = fbuf[g % 2, :, :, c0:c1].reshape(z.lines, c1 - c0)
                hi, lo = split(w)
                wh[g, :, c0:c1] = hi
                wl[g, :, c0:c1] = lo
                r = dot(duals[g], hi)
                r = r[: z.hours] + r[z.hours :] + dot(duals[g, : z.hours], lo)
                for p in range(c0 // LANES, c1 // LANES):
                    parts_r[g * (z.pairs + 1) + p] = r[:, p * LANES - c0 : (p + 1) * LANES - c0]
            return carry

        lax.fori_loop(0, z.groups, group, 0)

    def collect(m):
        found = []
        for k in range(2):
            for i in range(2):
                x = jnp.zeros((z.hours, LANES), f32)
                for g in range(z.groups):
                    x = x + parts_r[tab[(k * z.blocks + m * 2 + i) * z.groups + g]]
                found.append(x)
        low0, low1, high0, high1 = found
        crossed = jnp.where(low, low1, high0)
        img[m] = jnp.where(low, low0, high1) + pltpu.roll(crossed, z.cols, 1)

    others = z.parts - 1

    def img_copy(s, t):
        i = (s - 1) * half + t
        return pltpu.make_async_remote_copy(
            src_ref=img.at[s * half + t],
            dst_ref=img_in.at[i],
            send_sem=xsem.at[i],
            recv_sem=xsem.at[others * half + i],
            device_id=(me, (net + s) % z.parts),
            device_id_type=MESH,
        )

    def inj_copy(s, t):
        i = (s - 1) * half + t
        return pltpu.make_async_remote_copy(
            src_ref=inj.at[t],
            dst_ref=inj_in.at[i],
            send_sem=xsem.at[2 * others * half + i],
            recv_sem=xsem.at[3 * others * half + i],
            device_id=(me, (net - s + z.parts) % z.parts),
            device_id_type=MESH,
        )

    def each(fn):
        def one(i, carry):
            fn(i // half + 1, i % half)
            return carry

        lax.fori_loop(0, others * half, one, 0)

    def all_sent():
        each(lambda s, t: img_copy(s, t).wait_send())
        each(lambda s, t: inj_copy(s, t).wait_send())

    def hold(m, x):
        turned = pltpu.roll(x, z.cols, 1)
        zero = jnp.zeros_like(x)
        held[0, 2 * m] = stacked(jnp.where(low, x, zero))
        held[1, 2 * m] = stacked(jnp.where(low, zero, turned))
        held[0, 2 * m + 1] = stacked(jnp.where(low, turned, zero))
        held[1, 2 * m + 1] = stacked(jnp.where(low, zero, x))

    def dispatch(q):
        even = q % 2 == 0
        tile = (q // 2) * LANES

        def packed(ref, t):
            x = ref[:, pl.ds(pl.multiple_of((2 * t) * z.width + tile, LANES), LANES)]
            y = ref[:, pl.ds(pl.multiple_of((2 * t + 1) * z.width + tile, LANES), LANES)]
            here = lax.broadcasted_iota(jnp.int32, x.shape, 1) < z.cols
            keep = jnp.where(even, x, y)
            turn = pltpu.roll(jnp.where(even, y, x), z.cols, 1)
            return jnp.where(here == even, keep, turn)

        def pair(t, carry):
            image_t = img[t]
            for s in range(1, z.parts):
                img_copy(s, t).wait_recv()
                image_t = image_t + img_in[(s - 1) * half + t]
            price_t = level[...] + image_t
            gen_t = packed(gen, t)
            moved = jnp.maximum(
                gen_t - primal_step * (packed(fuel, t) + price_t + packed(head, t)), 0.0
            )
            turned = pltpu.roll(moved, z.cols, 1)
            for i in range(2):
                cols = pl.ds(pl.multiple_of((2 * t + i) * z.width + tile, LANES), LANES)
                mine = jnp.where(even, moved if i == 0 else turned, turned if i == 0 else moved)
                next_gen[:, cols] = jnp.where(low == even, mine, next_gen[:, cols])
            units = pl.ds(pl.multiple_of(t * LANES, LANES), LANES)
            row = lax.broadcasted_iota(jnp.int32, (LANES, LANES), 0).astype(f32)
            marks = jnp.where(row == place[q, :, units], 1.0, 0.0).astype(bf16)
            hi, lo = split(price_t)
            cost = price[:, units] + (dot(hi, marks) + dot(lo, marks))
            price[:, units] = cost
            b = back[:, units]
            cap = power[:, units]
            c, d = chg[:, units], dis[:, units]
            new_c = jnp.minimum(jnp.maximum(c - store_step * (efficiency * b - cost), 0.0), cap)
            new_d = jnp.minimum(jnp.maximum(d - store_step * (cost - b / efficiency), 0.0), cap)
            next_c[:, units] = new_c
            next_d[:, units] = new_d
            hi, lo = split((2.0 * new_d - d) - (2.0 * new_c - c))
            inj[t] = (2.0 * moved - gen_t) + (dot_t(hi, marks) + dot_t(lo, marks))
            for s in range(1, z.parts):
                inj_copy(s, t).start()
            return carry

        lax.fori_loop(0, half, pair, 0)

    def hold_own(t, carry):
        x = inj[t]
        total[...] += x
        hold(t, x)
        return carry

    def hold_in(s, t):
        inj_copy(s, t).wait_recv()
        x = inj_in[(s - 1) * half + t]
        total[...] += x
        hold(s * half + t, x)

    def flow(q, g):
        cols = pl.ds(pl.multiple_of(g * z.lines, z.lines), z.lines)
        both = []
        for p in range(z.pairs):
            x = None
            for k in range(2):
                if 2 * p + k < z.slots:
                    m = lax.rem(pat[g, 2 * p + k] - net * z.groups + z.blocks, z.blocks)
                    y = held[k, m]
                    x = y if x is None else x + y
            both.append(x)
        both = jnp.concatenate(both, axis=1)
        r = dot_t(both, wh[g])
        r = r[: z.hours] + r[z.hours :] + dot_t(both[: z.hours], wl[g])
        r = acc[:, cols] + r

        @pl.when(q < z.chunks - 1)
        def _():
            acc[:, cols] = r

        @pl.when(q == z.chunks - 1)
        def _():
            moved = line[:, cols] + dual_step * r
            floor = -limit[:, cols] - base[:, cols]
            ceiling = limit[:, cols] - base[:, cols]
            acc[:, cols] = moved - dual_step * jnp.minimum(
                jnp.maximum(moved / dual_step, floor), ceiling
            )
            line_out(g).start()


    def line_out(g):
        cols = pl.ds(pl.multiple_of(g * z.lines, z.lines), z.lines)
        return pltpu.make_async_copy(acc.at[:, cols], out_line.at[:, cols], osem.at[g])

    results = [
        pltpu.make_async_copy(v, h, osem.at[z.groups + i])
        for i, (v, h) in enumerate(
            [
                (next_gen, out_gen), (next_c, out_c), (next_d, out_d), (next_p, out_p),
                (next_s, out_s), (next_h, out_h), (next_e, out_e), (next_f, out_f),
            ]
        )
    ]

    def settle():
        for c in results[:3]:
            c.start()
        found = sums[z.rounds]
        next_plant = jnp.maximum(
            plant[...] - primal_step * (plant_cost[...] - found[:, : z.nodes] / (z.scen * z.hours)), 0.0
        )
        next_store = jnp.maximum(
            stored[...] - primal_step * (store_cost[...] - found[:, z.nodes :] / (z.scen * z.hours)), 0.0
        )
        next_p[...] = next_plant
        next_s[...] = next_store
        extra_plant = 2.0 * next_plant - plant[...]
        extra_store = 2.0 * next_store - stored[...]
        next_h[...] = jnp.maximum(
            head[...] + dual_step * ((2.0 * next_gen[...] - gen[...]) - avail[...] * extra_plant), 0.0
        )
        for c in results[3:6]:
            c.start()
        extra_c = 2.0 * next_c[...] - chg[...]
        extra_d = 2.0 * next_d[...] - dis[...]
        levels = decayed_sums(efficiency * extra_c - extra_d / efficiency, 1.0 - loss[...], False)
        next_e[...] = jnp.minimum(empty[...] + level_step * levels, 0.0)
        next_f[...] = jnp.maximum(dfull[...] + level_step * (levels - extra_store), 0.0)
        for c in results[6:]:
            c.start()

    steps = z.a
    points = 3

    def event(k, t):
        q = k - t // points

        def act():
            if t == 0:
                pl.when(q > 0)(lambda: begin(q))
            else:
                ga.step(q, t - 1)
            if t == steps:
                ga.finish(q)
                own_copy(q).wait()

        pl.when(jnp.logical_and(q >= 0, q < z.chunks))(act)

    ready = steps // points
    turn = steps % points

    def make_image(q):
        pl.when(q > 0)(all_sent)
        image(q)

        def send(s, t):
            collect(s * half + t)
            img_copy(s, t).start()

        each(send)
        pl.loop(0, half)(collect)

    def make_dispatch(q):
        dispatch(q)
        lax.fori_loop(0, half, hold_own, 0)
        pl.when(q == z.chunks - 1)(settle)
        ga.drain(q)

    def make_flows(q):
        each(hold_in)
        pl.loop(0, z.groups)(functools.partial(flow, q))

    tasks = [[] for _ in range(points)]
    for i, task in enumerate((make_image, make_dispatch, make_flows)):
        tasks[(turn + i) % points].append((ready + (turn + i) // points, task))

    def beat(k, carry):
        for o in range(points):
            for r in range(1, z.rounds + 1):
                if r % points == o:
                    @pl.when(k == r // points)
                    def _():
                        sum_copy(r - 1).wait_recv()
                        sums[r] = sums[r - 1] + sums_in[r - 1]
                        if r < z.rounds:
                            sum_copy(r).start()

            for t in range(o, steps + 1, points):
                event(k, t)
            if o == 0:
                pl.when(k == 0)(prepare_sums)
            if o == 1:
                pl.when(k == 0)(prepare_tables)
            for late, task in tasks[o]:
                q = k - late
                pl.when(jnp.logical_and(q >= 0, q < z.chunks))(functools.partial(task, q))
        return carry

    lax.fori_loop(0, z.chunks + ready + (turn + 2) // points, beat, 0)

    col_total = jnp.sum(total[...], axis=1, keepdims=True)
    row_total = jnp.sum(jnp.where(eye, col_total, 0.0), axis=0, keepdims=True)
    out_b[...] = balance[...] + dual_step * (row_total / (z.blocks * z.width) - demand[...])
    all_sent()
    for r in range(z.rounds):
        sum_copy(r).wait_send()
    for c in results:
        c.wait()
    for g in range(z.groups):
        line_out(g).wait()


def hand_on(n, *refs):
    held, into, out = refs[2 * n : 3 * n], refs[3 * n], refs[3 * n + 1]
    loads = [pltpu.make_async_copy(refs[i], held[i], into.at[i]) for i in range(n)]
    stores = [pltpu.make_async_copy(held[i], refs[n + i], out.at[i]) for i in range(n)]
    for c in loads:
        c.start()
    for a, b in zip(loads, stores):
        a.wait()
        b.start()
    for c in stores:
        c.wait()


def run_step(z, pat, big, small):
    h, n, st, ln = z.hours, z.nodes, z.stores, z.groups * z.lines
    half = z.groups // z.per
    others = z.parts - 1
    hbm = pl.BlockSpec(memory_space=pltpu.HBM)
    vmem = pl.BlockSpec(memory_space=pltpu.VMEM)
    smem = pl.BlockSpec(memory_space=pltpu.SMEM)

    def shape(*dims):
        return jax.ShapeDtypeStruct(dims, f32)

    def buffer(*dims, dtype=f32):
        return pltpu.VMEM(dims, dtype)

    outs = [
        shape(z.chunks, z.scen, z.rows, z.wide), shape(h, n), shape(h, st), shape(h, st),
        shape(1, n), shape(1, st), shape(h, ln), shape(h, n), shape(h, st), shape(h, st), shape(1, h),
    ]
    return pl.pallas_call(
        functools.partial(step_kernel, z),
        out_shape=outs,
        in_specs=[smem] + [hbm] * len(big) + [vmem] * len(small),
        out_specs=[hbm] * (len(outs) - 1) + [vmem],
        scratch_shapes=[
            buffer(z.groups, 2 * h, z.lines, dtype=bf16),
            buffer(z.groups, z.lines, z.wide, dtype=bf16),
            buffer(z.groups, z.lines, z.wide, dtype=bf16),
            buffer(2, z.scen, z.lines_local, z.wide),
            buffer(z.groups, z.slots, z.lines_local, z.width),
            buffer(z.chunks, z.rows, z.wide),
            buffer(z.groups * (z.pairs + 1), h, LANES),
            buffer(z.parts * half, h, LANES),
            buffer(others * half, h, LANES),
            buffer(half, h, LANES),
            buffer(others * half, h, LANES),
            buffer(2, z.blocks, 2 * h, LANES, dtype=bf16),
            buffer(h, ln),
            buffer(h, ln),
        ]
        + [buffer(h, n)] * 3
        + [buffer(h, st)] * 10
        + [
            buffer(z.chunks, 1, st),
            buffer(h, LANES),
            buffer(z.rounds + 1, 1, n + st),
            buffer(z.rounds, 1, n + st),
            buffer(h, ln),
            buffer(h, n),
            buffer(h, n),
            buffer(1, n),
            buffer(1, st),
            buffer(h, LANES),
            pltpu.SMEM((2 * z.blocks * z.groups,), jnp.int32),
            pltpu.SemaphoreType.DMA((z.chunks * 2 * (z.scen // 2) * 5,)),
            pltpu.SemaphoreType.DMA((z.chunks * 2 * z.scen,)),
            pltpu.SemaphoreType.DMA((2,)),
            pltpu.SemaphoreType.DMA((4 * others * half,)),
            pltpu.SemaphoreType.DMA((len(big) + z.chunks,)),
            pltpu.SemaphoreType.DMA((2 * z.rounds,)),
            pltpu.SemaphoreType.DMA((z.groups + 8,)),
        ],
        compiler_params=pltpu.CompilerParams(
            vmem_limit_bytes=VMEM_BYTES, collective_id=0, has_side_effects=True
        ),
        cost_estimate=pl.CostEstimate(
            flops=12 * h * z.groups * z.lines * z.slots * z.width,
            bytes_accessed=12 * z.groups * z.lines * z.slots * z.width,
            transcendentals=0,
        ),
        name="iteration",
    )(pat, *big, *small)


def body(
    generation, charging, discharging, plant_capacity, store_capacity, dual_balance, dual_line,
    dual_headroom, dual_empty, dual_full, availability, demand, line_base, line_limit, fuel_cost,
    plant_cost, store_cost, self_loss, power_limit, store_node, line_factors, block_pattern,
):
    z = Sizes(lax.axis_size("scen"), lax.axis_size("net"), generation, line_factors, store_node)
    big = [
        line_factors.transpose(0, 2, 1, 3), dual_line[0], line_base[0], generation[0],
        dual_headroom[0], availability[0], charging[0], discharging[0], dual_empty[0], dual_full[0],
    ]
    small = [dual_balance, demand] + [
        x[None]
        for x in (
            fuel_cost, self_loss, power_limit, store_node, line_limit,
            plant_capacity, plant_cost, store_capacity, store_cost,
        )
    ]
    outs = run_step(z, block_pattern, big, small)[1:]
    hbm = pl.BlockSpec(memory_space=pltpu.HBM)
    gen, chg, dis, plant, stored, line, head, empty, full, balance = pl.pallas_call(
        functools.partial(hand_on, len(outs)),
        out_shape=[jax.ShapeDtypeStruct(x.shape, x.dtype) for x in outs],
        in_specs=[hbm] * len(outs),
        out_specs=[hbm] * len(outs),
        scratch_shapes=[pltpu.VMEM(x.shape, x.dtype) for x in outs]
        + [pltpu.SemaphoreType.DMA((len(outs),))] * 2,
        compiler_params=pltpu.CompilerParams(vmem_limit_bytes=VMEM_BYTES),
        name="results",
    )(*outs)
    return (
        gen[None], chg[None], dis[None], plant[0], stored[0], balance,
        line[None], head[None], empty[None], full[None],
    )


def solution(mesh):
    row = P("scen", None, "net")
    placed = (
        row, row, row, P("net"), P("net"), P("scen", None), row, row, row, row, row,
        P("scen", None), row, P("net"), P("net"), P("net"), P("net"), P("net"), P("net"), P("net"),
        P("net", "scen", None, None), P("net", None),
    )
    return jax.shard_map(
        body,
        mesh=mesh,
        in_specs=placed,
        out_specs=(row, row, row, P("net"), P("net"), P("scen", None), row, row, row, row),
        check_vma=False,
    )
```

```python
import functools

import jax
import jax.numpy as jnp
from jax import lax
from jax.experimental import pallas as pl
from jax.experimental.pallas import tpu as pltpu
from jax.sharding import PartitionSpec as P

LANES = 128
primal_step = 0.5
dual_step = 0.5
store_step = 0.05
level_step = 0.05
efficiency = 0.92
f32 = jnp.float32
bf16 = jnp.bfloat16
VMEM_BYTES = 56 * 1024 * 1024
MESH = pl.DeviceIdType.MESH
UP, DOWN, RIGHT, LEFT, CORE = range(5)


def split(x):
    hi = x.astype(bf16)
    return hi, (x - hi.astype(f32)).astype(bf16)


def stacked(x):
    return jnp.concatenate([x, x - x.astype(bf16).astype(f32)], axis=0).astype(bf16)


def dot(a, b):
    return jnp.dot(a, b, preferred_element_type=f32)


def dot_t(a, b):
    return lax.dot_general(a, b, (((1,), (1,)), ((), ())), preferred_element_type=f32)


def decayed_sums(x, keep, reverse):
    hours = x.shape[0]
    hour = lax.broadcasted_iota(jnp.int32, x.shape, 0)
    power = keep
    lag = 1
    while lag < hours:
        if reverse:
            moved = jnp.where(hour < hours - lag, pltpu.roll(x, hours - lag, 0), 0.0)
        else:
            moved = jnp.where(hour >= lag, pltpu.roll(x, lag, 0), 0.0)
        x = x + power * moved
        power = power * power
        lag *= 2
    return x


def when_all(conds, fn):
    if not conds:
        fn()
        return
    c = conds[0]
    for d in conds[1:]:
        c = jnp.logical_and(c, d)
    pl.when(c)(fn)


class Sizes:
    def __init__(self, scen, parts, generation, line_factors, store_node):
        _, self.hours, self.nodes = generation.shape
        self.groups, self.lines_local, self.slots, self.width = line_factors.shape
        self.scen, self.parts = scen, parts
        self.stores = store_node.shape[0]
        self.per = LANES // (self.stores // self.groups)
        assert self.per == 2
        self.cols = LANES // self.per
        self.chunks = self.width // self.cols
        self.pairs = -(-self.slots // self.per)
        self.wide = self.pairs * LANES
        self.lines = scen * self.lines_local
        self.rows = self.groups * self.lines_local
        self.blocks = self.groups * parts
        cut = -(-self.rows * 5 // 32 // 8) * 8
        self.cuts = ((0, self.rows - cut), (self.rows - cut, cut))
        plane = scen // 2
        self.rounds = scen.bit_length() - 1
        assert 2**self.rounds == scen
        self.b = max(d for d in range(1, plane + 1) if plane % d == 0 and d * d <= plane)
        self.a = plane // self.b


class Gather:
    def __init__(self, z, own, full, ssem, rsem):
        self.z, self.own, self.full, self.ssem, self.rsem = z, own, full, ssem, rsem
        self.me = lax.axis_index("scen")
        self.net = lax.axis_index("net")
        self.c = self.me % 2
        self.ib = (self.me // 2) % z.b
        self.ia = self.me // (2 * z.b)

    def slot(self, a, b):
        return (a * self.z.b + b) * 2 + self.c

    def has(self, way):
        return {
            UP: [self.ia < self.z.a - 1],
            DOWN: [self.ia > 0],
            RIGHT: [self.ib < self.z.b - 1],
            LEFT: [self.ib > 0],
            CORE: [],
        }[way]

    def device(self, way):
        z = self.z
        step = {UP: 2 * z.b, DOWN: -2 * z.b, RIGHT: 2, LEFT: -2}
        to = self.me + 1 - 2 * self.c if way == CORE else self.me + step[way]
        return (to, self.net)

    def copy(self, q, part, slot, way, own):
        start, size = self.z.cuts[part]
        rows = pl.ds(start, size)
        src = self.own.at[q, rows] if own else self.full.at[q, slot, rows]
        item = ((q * 2 + part) * (self.z.scen // 2) + slot // 2) * 5 + way
        return pltpu.make_async_remote_copy(
            src_ref=src,
            dst_ref=self.full.at[q, slot, rows],
            send_sem=self.ssem.at[item],
            recv_sem=self.rsem.at[(q * 2 + part) * self.z.scen + slot],
            device_id=self.device(way),
            device_id_type=MESH,
        )

    def arrivals(self):
        na, nb = self.z.a, self.z.b
        span = [0] + [s * k for k in range(1, na) for s in (-1, 1)]
        side = [0] + [s * k for k in range(1, nb) for s in (-1, 1)]
        steps = [[] for _ in range(na + 1)]
        for t in range(na - 1):
            for s, way in ((-1, UP), (1, DOWN)):
                steps[t].append((0, s * (t + 1), 0, [way, RIGHT, LEFT, CORE]))
        for u in range(nb - 1):
            for s, way in ((-1, RIGHT), (1, LEFT)):
                steps[min(u, na - 1)].append((1, 0, s * (u + 1), [way, UP, DOWN, CORE]))
        for t in range(na - 1):
            for e in side:
                for s, way in ((-1, UP), (1, DOWN)):
                    steps[min(na, t + abs(e))].append((1, s * (t + 1), e, [way, CORE]))
        for u in range(nb - 1):
            for d in span:
                for s, way in ((-1, RIGHT), (1, LEFT)):
                    steps[min(na, abs(d) + u + 1)].append((0, d, s * (u + 1), [way, CORE]))
        return steps

    def valid(self, d, e):
        out = []
        if d < 0:
            out.append(self.ia + d >= 0)
        if d > 0:
            out.append(self.ia + d < self.z.a)
        if e < 0:
            out.append(self.ib + e >= 0)
        if e > 0:
            out.append(self.ib + e < self.z.b)
        return out

    def start_own(self, q):
        for part in range(2):
            for way in (UP, DOWN, RIGHT, LEFT, CORE):
                when_all(
                    self.has(way),
                    lambda: self.copy(q, part, self.me, way, True).start(),
                )

    def step(self, q, t):
        for part, d, e, ways in self.arrivals()[t]:
            def arrive(part=part, d=d, e=e, ways=ways):
                slot = self.slot(self.ia + d, self.ib + e)
                self.copy(q, part, slot, CORE, False).wait_recv()
                for way in ways:
                    when_all(
                        self.has(way),
                        lambda: self.copy(q, part, slot, way, False).start(),
                    )
            when_all(self.valid(d, e), arrive)

    def finish(self, q):
        def one(i, carry):
            for part in range(2):
                self.copy(q, part, 2 * i + 1 - self.c, CORE, False).wait_recv()
            return carry
        lax.fori_loop(0, self.z.scen // 2, one, 0)

    def drain(self, q):
        for part in range(2):
            for way in (UP, DOWN, RIGHT, LEFT, CORE):
                when_all(
                    self.has(way),
                    lambda: self.copy(q, part, self.me, way, True).wait_send(),
                )
        for step in self.arrivals():
            for part, d, e, ways in step:
                def sent(part=part, d=d, e=e, ways=ways):
                    slot = self.slot(self.ia + d, self.ib + e)
                    for way in ways:
                        when_all(
                            self.has(way),
                            lambda: self.copy(q, part, slot, way, False).wait_send(),
                        )
                when_all(self.valid(d, e), sent)


def step_kernel(
    z, pat, fac_h, line_h, base_h, gen_h, head_h, avail_h, chg_h, dis_h, empty_h, full_h,
    balance, demand, fuel, loss, power, node, limit, plant, plant_cost, stored, store_cost,
    full, out_gen, out_c, out_d, out_p, out_s, out_line, out_h, out_e, out_f, out_b,
    duals, wh, wl, fbuf, fac, own, parts_r, img, img_in, inj, inj_in, held,
    line, base, gen, head, avail, chg, dis, empty, dfull, back, price, next_c, next_d, next_e, next_f,
    place, total, sums, sums_in, acc, next_gen, next_h, next_p, next_s, level, tab,
    ssem, rsem, fsem, xsem, msem, tsem, osem,
):
    me, net = lax.axis_index("scen"), lax.axis_index("net")
    half = z.groups // z.per
    lane = lax.broadcasted_iota(jnp.int32, (z.hours, LANES), 1)
    low = lane < z.cols
    ga = Gather(z, own, full, ssem, rsem)

    barrier = pltpu.get_barrier_semaphore()
    for way in (UP, DOWN, RIGHT, LEFT, CORE):
        when_all(
            ga.has(way),
            lambda: pl.semaphore_signal(
                barrier, inc=1, device_id=ga.device(way), device_id_type=MESH
            ),
        )
    for s in range(1, z.parts):
        pl.semaphore_signal(
            barrier, inc=1, device_id=(me, (net + s) % z.parts), device_id_type=MESH
        )

    def mate(r):
        bit = 2**r
        return (me + bit - 2 * bit * ((me // bit) % 2), net)

    for r in range(z.rounds):
        pl.semaphore_signal(barrier, inc=1, device_id=mate(r), device_id_type=MESH)
    met = jnp.int32(z.parts + z.rounds)
    for way in (UP, DOWN, RIGHT, LEFT):
        for c in ga.has(way):
            met = met + c.astype(jnp.int32)

    loads = [
        pltpu.make_async_copy(h, v, msem.at[i])
        for i, (h, v) in enumerate(
            [
                (fac_h, fac), (line_h, line), (empty_h, empty), (full_h, dfull), (head_h, head),
                (avail_h, avail), (gen_h, gen), (chg_h, chg), (dis_h, dis), (base_h, base),
            ]
        )
    ]
    for c in loads:
        c.start()

    def own_copy(q):
        return pltpu.make_async_copy(own.at[q], full.at[q, me], msem.at[len(loads) + q])

    def lay_out(q):
        even = q % 2 == 0
        tile = pl.ds(pl.multiple_of((q // 2) * LANES, LANES), LANES)
        here = lax.broadcasted_iota(jnp.int32, (z.lines_local, LANES), 1) < z.cols
        for g in range(z.groups):
            for p in range(z.pairs):
                x = fac[g, 2 * p, :, tile]
                y = fac[g, 2 * p + 1, :, tile] if 2 * p + 1 < z.slots else jnp.zeros_like(x)
                keep = jnp.where(even, x, y)
                turn = pltpu.roll(jnp.where(even, y, x), z.cols, 1)
                own[q, g * z.lines_local : (g + 1) * z.lines_local, p * LANES : (p + 1) * LANES] = (
                    jnp.where(here == even, keep, turn)
                )

    def begin(q):
        lay_out(q)
        ga.start_own(q)
        own_copy(q).start()

    def sum_copy(r):
        return pltpu.make_async_remote_copy(
            src_ref=sums.at[r],
            dst_ref=sums_in.at[r],
            send_sem=tsem.at[r],
            recv_sem=tsem.at[z.rounds + r],
            device_id=mate(r),
            device_id_type=MESH,
        )

    loads[0].wait()
    lay_out(0)
    pl.semaphore_wait(barrier, met)
    ga.start_own(0)
    own_copy(0).start()

    hour_r = lax.broadcasted_iota(jnp.int32, (z.hours, z.hours), 0)
    hour_c = lax.broadcasted_iota(jnp.int32, (z.hours, z.hours), 1)
    eye = hour_r == hour_c

    def take_line(g, carry):
        cols = pl.ds(pl.multiple_of(g * z.lines, z.lines), z.lines)
        duals[g] = stacked(line[:, cols])
        parts_r[g * (z.pairs + 1) + z.pairs] = jnp.zeros((z.hours, LANES), f32)
        return carry

    def find(m, carry):
        def in_group(g, carry):
            for k in range(2):
                found = jnp.int32(z.pairs)
                for p in range(z.pairs):
                    j = 2 * p + k
                    if j < z.slots:
                        block = lax.rem(pat[g, j] - net * z.groups + z.blocks, z.blocks)
                        found = jnp.where(block == m, p, found)
                tab[(k * z.blocks + m) * z.groups + g] = g * (z.pairs + 1) + found
            return carry

        return lax.fori_loop(0, z.groups, in_group, carry)

    def prepare_sums():
        for c in loads[1:]:
            c.wait()
        sums[0, :, : z.nodes] = jnp.sum(avail[...] * head[...], axis=0, keepdims=True)
        sums[0, :, z.nodes :] = jnp.sum(dfull[...], axis=0, keepdims=True)
        sum_copy(0).start()
        price[...] = jnp.zeros_like(price)
        total[...] = jnp.zeros_like(total)
        acc[...] = jnp.zeros_like(acc)
        lax.fori_loop(0, z.groups, take_line, 0)

    def prepare_tables():
        lax.fori_loop(0, z.blocks, find, 0)
        at = (node[...] - net * z.nodes).astype(f32)
        block = jnp.floor((at + 0.5) / z.width)
        col = at - block * z.width
        unit = lax.broadcasted_iota(jnp.int32, at.shape, 1).astype(f32)
        pair_of = jnp.floor((unit + 0.5) / LANES)
        part_of = jnp.floor((col + 0.5) / z.cols)
        spot = (block - pair_of * z.per) * z.cols + col - part_of * z.cols
        for q in range(z.chunks):
            place[q] = jnp.where(part_of == q, spot, -1.0)
        back[...] = decayed_sums(empty[...] + dfull[...], 1.0 - loss[...], True)
        column = jnp.sum(jnp.where(eye, balance[...], 0.0), axis=1, keepdims=True)
        level[...] = jnp.broadcast_to(column, level.shape)

    def factor_copy(q, g):
        return pltpu.make_async_copy(
            full.at[q, :, pl.ds(pl.multiple_of(g * z.lines_local, 8), z.lines_local)],
            fbuf.at[g % 2], fsem.at[g % 2],
        )

    def image(q):
        factor_copy(q, 0).start()

        def group(g, carry):
            factor_copy(q, g).wait()

            @pl.when(g + 1 < z.groups)
            def _():
                factor_copy(q, g + 1).start()

            for c0 in range(0, z.wide, 2 * LANES):
                c1 = min(c0 + 2 * LANES, z.wide)
                w = fbuf[g % 2, :, :, c0:c1].reshape(z.lines, c1 - c0)
                hi, lo = split(w)
                wh[g, :, c0:c1] = hi
                wl[g, :, c0:c1] = lo
                r = dot(duals[g], hi)
                r = r[: z.hours] + r[z.hours :] + dot(duals[g, : z.hours], lo)
                for p in range(c0 // LANES, c1 // LANES):
                    parts_r[g * (z.pairs + 1) + p] = r[:, p * LANES - c0 : (p + 1) * LANES - c0]
            return carry

        lax.fori_loop(0, z.groups, group, 0, unroll=2)

    def collect(m):
        found = []
        for k in range(2):
            for i in range(2):
                x = jnp.zeros((z.hours, LANES), f32)
                for g in range(z.groups):
                    x = x + parts_r[tab[(k * z.blocks + m * 2 + i) * z.groups + g]]
                found.append(x)
        low0, low1, high0, high1 = found
        crossed = jnp.where(low, low1, high0)
        img[m] = jnp.where(low, low0, high1) + pltpu.roll(crossed, z.cols, 1)

    others = z.parts - 1

    def img_copy(s, t):
        i = (s - 1) * half + t
        return pltpu.make_async_remote_copy(
            src_ref=img.at[s * half + t],
            dst_ref=img_in.at[i],
            send_sem=xsem.at[i],
            recv_sem=xsem.at[others * half + i],
            device_id=(me, (net + s) % z.parts),
            device_id_type=MESH,
        )

    def inj_copy(s, t):
        i = (s - 1) * half + t
        return pltpu.make_async_remote_copy(
            src_ref=inj.at[t],
            dst_ref=inj_in.at[i],
            send_sem=xsem.at[2 * others * half + i],
            recv_sem=xsem.at[3 * others * half + i],
            device_id=(me, (net - s + z.parts) % z.parts),
            device_id_type=MESH,
        )

    def each(fn):
        def one(i, carry):
            fn(i // half + 1, i % half)
            return carry

        lax.fori_loop(0, others * half, one, 0)

    def all_sent():
        each(lambda s, t: img_copy(s, t).wait_send())
        each(lambda s, t: inj_copy(s, t).wait_send())

    def hold(m, x):
        turned = pltpu.roll(x, z.cols, 1)
        zero = jnp.zeros_like(x)
        held[0, 2 * m] = stacked(jnp.where(low, x, zero))
        held[1, 2 * m] = stacked(jnp.where(low, zero, turned))
        held[0, 2 * m + 1] = stacked(jnp.where(low, turned, zero))
        held[1, 2 * m + 1] = stacked(jnp.where(low, zero, x))

    def dispatch(q):
        even = q % 2 == 0
        tile = (q // 2) * LANES

        def packed(ref, t):
            x = ref[:, pl.ds(pl.multiple_of((2 * t) * z.width + tile, LANES), LANES)]
            y = ref[:, pl.ds(pl.multiple_of((2 * t + 1) * z.width + tile, LANES), LANES)]
            here = lax.broadcasted_iota(jnp.int32, x.shape, 1) < z.cols
            keep = jnp.where(even, x, y)
            turn = pltpu.roll(jnp.where(even, y, x), z.cols, 1)
            return jnp.where(here == even, keep, turn)

        def pair(t, carry):
            image_t = img[t]
            for s in range(1, z.parts):
                img_copy(s, t).wait_recv()
                image_t = image_t + img_in[(s - 1) * half + t]
            price_t = level[...] + image_t
            gen_t = packed(gen, t)
            moved = jnp.maximum(
                gen_t - primal_step * (packed(fuel, t) + price_t + packed(head, t)), 0.0
            )
            turned = pltpu.roll(moved, z.cols, 1)
            for i in range(2):
                cols = pl.ds(pl.multiple_of((2 * t + i) * z.width + tile, LANES), LANES)
                mine = jnp.where(even, moved if i == 0 else turned, turned if i == 0 else moved)
                next_gen[:, cols] = jnp.where(low == even, mine, next_gen[:, cols])
            units = pl.ds(pl.multiple_of(t * LANES, LANES), LANES)
            row = lax.broadcasted_iota(jnp.int32, (LANES, LANES), 0).astype(f32)
            marks = jnp.where(row == place[q, :, units], 1.0, 0.0).astype(bf16)
            hi, lo = split(price_t)
            cost = price[:, units] + (dot(hi, marks) + dot(lo, marks))
            price[:, units] = cost
            b = back[:, units]
            cap = power[:, units]
            c, d = chg[:, units], dis[:, units]
            new_c = jnp.minimum(jnp.maximum(c - store_step * (efficiency * b - cost), 0.0), cap)
            new_d = jnp.minimum(jnp.maximum(d - store_step * (cost - b / efficiency), 0.0), cap)
            next_c[:, units] = new_c
            next_d[:, units] = new_d
            hi, lo = split((2.0 * new_d - d) - (2.0 * new_c - c))
            inj[t] = (2.0 * moved - gen_t) + (dot_t(hi, marks) + dot_t(lo, marks))
            for s in range(1, z.parts):
                inj_copy(s, t).start()
            return carry

        lax.fori_loop(0, half, pair, 0)

    def hold_own(t, carry):
        x = inj[t]
        total[...] += x
        hold(t, x)
        return carry

    def hold_in(s, t):
        inj_copy(s, t).wait_recv()
        x = inj_in[(s - 1) * half + t]
        total[...] += x
        hold(s * half + t, x)

    def flow(q, g):
        cols = pl.ds(pl.multiple_of(g * z.lines, z.lines), z.lines)
        both = []
        for p in range(z.pairs):
            x = None
            for k in range(2):
                if 2 * p + k < z.slots:
                    m = lax.rem(pat[g, 2 * p + k] - net * z.groups + z.blocks, z.blocks)
                    y = held[k, m]
                    x = y if x is None else x + y
            both.append(x)
        both = jnp.concatenate(both, axis=1)
        r = dot_t(both, wh[g])
        r = r[: z.hours] + r[z.hours :] + dot_t(both[: z.hours], wl[g])
        r = acc[:, cols] + r

        @pl.when(q < z.chunks - 1)
        def _():
            acc[:, cols] = r

        @pl.when(q == z.chunks - 1)
        def _():
            moved = line[:, cols] + dual_step * r
            floor = -limit[:, cols] - base[:, cols]
            ceiling = limit[:, cols] - base[:, cols]
            acc[:, cols] = moved - dual_step * jnp.minimum(
                jnp.maximum(moved / dual_step, floor), ceiling
            )
            line_out(g).start()


    def line_out(g):
        cols = pl.ds(pl.multiple_of(g * z.lines, z.lines), z.lines)
        return pltpu.make_async_copy(acc.at[:, cols], out_line.at[:, cols], osem.at[g])

    results = [
        pltpu.make_async_copy(v, h, osem.at[z.groups + i])
        for i, (v, h) in enumerate(
            [
                (next_gen, out_gen), (next_c, out_c), (next_d, out_d), (next_p, out_p),
                (next_s, out_s), (next_h, out_h), (next_e, out_e), (next_f, out_f),
            ]
        )
    ]

    def settle():
        for c in results[:3]:
            c.start()
        found = sums[z.rounds]
        next_plant = jnp.maximum(
            plant[...] - primal_step * (plant_cost[...] - found[:, : z.nodes] / (z.scen * z.hours)), 0.0
        )
        next_store = jnp.maximum(
            stored[...] - primal_step * (store_cost[...] - found[:, z.nodes :] / (z.scen * z.hours)), 0.0
        )
        next_p[...] = next_plant
        next_s[...] = next_store
        extra_plant = 2.0 * next_plant - plant[...]
        extra_store = 2.0 * next_store - stored[...]
        next_h[...] = jnp.maximum(
            head[...] + dual_step * ((2.0 * next_gen[...] - gen[...]) - avail[...] * extra_plant), 0.0
        )
        for c in results[3:6]:
            c.start()
        extra_c = 2.0 * next_c[...] - chg[...]
        extra_d = 2.0 * next_d[...] - dis[...]
        levels = decayed_sums(efficiency * extra_c - extra_d / efficiency, 1.0 - loss[...], False)
        next_e[...] = jnp.minimum(empty[...] + level_step * levels, 0.0)
        next_f[...] = jnp.maximum(dfull[...] + level_step * (levels - extra_store), 0.0)
        for c in results[6:]:
            c.start()

    steps = z.a + 1
    points = 3
    lead = 1

    def event(k, t):
        q = k - t // points if t else k + lead

        def act():
            if t == 0:
                begin(q)
            else:
                ga.step(q, t - 1)
            if t == steps:
                ga.finish(q)
                own_copy(q).wait()

        pl.when(jnp.logical_and(q >= 0, q < z.chunks))(act)

    ready = steps // points
    turn = steps % points

    def make_image(q):
        pl.when(q > 0)(all_sent)
        image(q)

        def send(s, t):
            collect(s * half + t)
            img_copy(s, t).start()

        each(send)
        pl.loop(0, half)(collect)

    def make_dispatch(q):
        dispatch(q)
        lax.fori_loop(0, half, hold_own, 0)
        pl.when(q == z.chunks - 1)(settle)
        ga.drain(q)

    def make_flows(q):
        each(hold_in)
        lax.fori_loop(0, z.groups, lambda g, c: (flow(q, g), c)[1], 0, unroll=2)

    tasks = [[] for _ in range(points)]
    for i, task in enumerate((make_image, make_dispatch, make_flows)):
        tasks[(turn + i) % points].append((ready + (turn + i) // points, task))

    def beat(k, carry):
        for o in range(points):
            for r in range(1, z.rounds + 1):
                if r % points == o:
                    @pl.when(k == r // points)
                    def _():
                        sum_copy(r - 1).wait_recv()
                        sums[r] = sums[r - 1] + sums_in[r - 1]
                        if r < z.rounds:
                            sum_copy(r).start()

            for t in reversed(range(o, steps + 1, points)):
                event(k, t)
            if o == 0:
                pl.when(k == 0)(prepare_sums)
            if o == 1:
                pl.when(k == 0)(prepare_tables)
            for late, task in tasks[o]:
                q = k - late
                pl.when(jnp.logical_and(q >= 0, q < z.chunks))(functools.partial(task, q))
        return carry

    lax.fori_loop(0, z.chunks + ready + (turn + 2) // points, beat, 0)

    col_total = jnp.sum(total[...], axis=1, keepdims=True)
    row_total = jnp.sum(jnp.where(eye, col_total, 0.0), axis=0, keepdims=True)
    out_b[...] = balance[...] + dual_step * (row_total / (z.blocks * z.width) - demand[...])
    all_sent()
    for r in range(z.rounds):
        sum_copy(r).wait_send()
    for c in results:
        c.wait()
    for g in range(z.groups):
        line_out(g).wait()


def hand_on(n, *refs):
    held, into, out = refs[2 * n : 3 * n], refs[3 * n], refs[3 * n + 1]
    loads = [pltpu.make_async_copy(refs[i], held[i], into.at[i]) for i in range(n)]
    stores = [pltpu.make_async_copy(held[i], refs[n + i], out.at[i]) for i in range(n)]
    for c in loads:
        c.start()
    for a, b in zip(loads, stores):
        a.wait()
        b.start()
    for c in stores:
        c.wait()


def run_step(z, pat, big, small):
    h, n, st, ln = z.hours, z.nodes, z.stores, z.groups * z.lines
    half = z.groups // z.per
    others = z.parts - 1
    hbm = pl.BlockSpec(memory_space=pltpu.HBM)
    vmem = pl.BlockSpec(memory_space=pltpu.VMEM)
    smem = pl.BlockSpec(memory_space=pltpu.SMEM)

    def shape(*dims):
        return jax.ShapeDtypeStruct(dims, f32)

    def buffer(*dims, dtype=f32):
        return pltpu.VMEM(dims, dtype)

    outs = [
        shape(z.chunks, z.scen, z.rows, z.wide), shape(h, n), shape(h, st), shape(h, st),
        shape(1, n), shape(1, st), shape(h, ln), shape(h, n), shape(h, st), shape(h, st), shape(1, h),
    ]
    return pl.pallas_call(
        functools.partial(step_kernel, z),
        out_shape=outs,
        in_specs=[smem] + [hbm] * len(big) + [vmem] * len(small),
        out_specs=[hbm] * (len(outs) - 1) + [vmem],
        scratch_shapes=[
            buffer(z.groups, 2 * h, z.lines, dtype=bf16),
            buffer(z.groups, z.lines, z.wide, dtype=bf16),
            buffer(z.groups, z.lines, z.wide, dtype=bf16),
            buffer(2, z.scen, z.lines_local, z.wide),
            buffer(z.groups, z.slots, z.lines_local, z.width),
            buffer(z.chunks, z.rows, z.wide),
            buffer(z.groups * (z.pairs + 1), h, LANES),
            buffer(z.parts * half, h, LANES),
            buffer(others * half, h, LANES),
            buffer(half, h, LANES),
            buffer(others * half, h, LANES),
            buffer(2, z.blocks, 2 * h, LANES, dtype=bf16),
            buffer(h, ln),
            buffer(h, ln),
        ]
        + [buffer(h, n)] * 3
        + [buffer(h, st)] * 10
        + [
            buffer(z.chunks, 1, st),
            buffer(h, LANES),
            buffer(z.rounds + 1, 1, n + st),
            buffer(z.rounds, 1, n + st),
            buffer(h, ln),
            buffer(h, n),
            buffer(h, n),
            buffer(1, n),
            buffer(1, st),
            buffer(h, LANES),
            pltpu.SMEM((2 * z.blocks * z.groups,), jnp.int32),
            pltpu.SemaphoreType.DMA((z.chunks * 2 * (z.scen // 2) * 5,)),
            pltpu.SemaphoreType.DMA((z.chunks * 2 * z.scen,)),
            pltpu.SemaphoreType.DMA((2,)),
            pltpu.SemaphoreType.DMA((4 * others * half,)),
            pltpu.SemaphoreType.DMA((len(big) + z.chunks,)),
            pltpu.SemaphoreType.DMA((2 * z.rounds,)),
            pltpu.SemaphoreType.DMA((z.groups + 8,)),
        ],
        compiler_params=pltpu.CompilerParams(
            vmem_limit_bytes=VMEM_BYTES, collective_id=0, has_side_effects=True
        ),
        cost_estimate=pl.CostEstimate(
            flops=12 * h * z.groups * z.lines * z.slots * z.width,
            bytes_accessed=12 * z.groups * z.lines * z.slots * z.width,
            transcendentals=0,
        ),
        name="iteration",
    )(pat, *big, *small)


def body(
    generation, charging, discharging, plant_capacity, store_capacity, dual_balance, dual_line,
    dual_headroom, dual_empty, dual_full, availability, demand, line_base, line_limit, fuel_cost,
    plant_cost, store_cost, self_loss, power_limit, store_node, line_factors, block_pattern,
):
    z = Sizes(lax.axis_size("scen"), lax.axis_size("net"), generation, line_factors, store_node)
    big = [
        line_factors.transpose(0, 2, 1, 3), dual_line[0], line_base[0], generation[0],
        dual_headroom[0], availability[0], charging[0], discharging[0], dual_empty[0], dual_full[0],
    ]
    small = [dual_balance, demand] + [
        x[None]
        for x in (
            fuel_cost, self_loss, power_limit, store_node, line_limit,
            plant_capacity, plant_cost, store_capacity, store_cost,
        )
    ]
    outs = run_step(z, block_pattern, big, small)[1:]
    hbm = pl.BlockSpec(memory_space=pltpu.HBM)
    gen, chg, dis, plant, stored, line, head, empty, full, balance = pl.pallas_call(
        functools.partial(hand_on, len(outs)),
        out_shape=[jax.ShapeDtypeStruct(x.shape, x.dtype) for x in outs],
        in_specs=[hbm] * len(outs),
        out_specs=[hbm] * len(outs),
        scratch_shapes=[pltpu.VMEM(x.shape, x.dtype) for x in outs]
        + [pltpu.SemaphoreType.DMA((len(outs),))] * 2,
        compiler_params=pltpu.CompilerParams(vmem_limit_bytes=VMEM_BYTES),
        name="results",
    )(*outs)
    return (
        gen[None], chg[None], dis[None], plant[0], stored[0], balance,
        line[None], head[None], empty[None], full[None],
    )


def solution(mesh):
    row = P("scen", None, "net")
    placed = (
        row, row, row, P("net"), P("net"), P("scen", None), row, row, row, row, row,
        P("scen", None), row, P("net"), P("net"), P("net"), P("net"), P("net"), P("net"), P("net"),
        P("net", "scen", None, None), P("net", None),
    )
    return jax.shard_map(
        body,
        mesh=mesh,
        in_specs=placed,
        out_specs=(row, row, row, P("net"), P("net"), P("scen", None), row, row, row, row),
        check_vma=False,
    )
```
